256 devices in a mesh: section: 8 (over z), expert: 32 (over y, x, core).
Axes of the slice: x: 4, y: 4, z: 8, core: 2. Of those that a mesh axis runs over, the one named last changes fastest.
Arguments:
- features: bfloat16 [2, 2048, 2048], P(None, 'expert'), may hold values from -6 to 6
- labels: int32 [2, 2048], P(None, 'expert'), may hold values 0 or 1
- routes: int32 [8, 2, 2048, 1], P('section', None, 'expert'), may hold values from 0 to 31; in each aligned block of 64 rows (0 to 63, 64 to 127, ..., all dimensions but the last counted through in order) at most 3 rows name the same one
- route_gates: float32 [8, 2, 2048], P('section', None, 'expert'), may hold values from 0.25 to 1
- gate_weight: bfloat16 [8, 32, 2048, 256], P('section', 'expert'), may hold values from -0.125 to 0.125
- up_weight: bfloat16 [8, 32, 2048, 256], P('section', 'expert'), may hold values from -0.125 to 0.125
- down_weight: bfloat16 [8, 32, 256, 2048], P('section', 'expert'), may hold values from -0.375 to 0.375
- lowrank_in: bfloat16 [8, 2048, 128], P('section'), may hold values from -0.125 to 0.125
- lowrank_out: bfloat16 [8, 128, 2048], P('section'), may hold values from -0.5 to 0.5
- head_weight: float32 [2048], replicated, may hold values from -0.5 to 0.5
Outputs:
- grad_gate: float32 [8, 32, 2048, 256], P('section', 'expert')
- grad_up: float32 [8, 32, 2048, 256], P('section', 'expert')
- grad_down: float32 [8, 32, 256, 2048], P('section', 'expert')
- grad_lowrank_in: float32 [8, 2048, 128], P('section', 'expert')
- grad_lowrank_out: float32 [8, 128, 2048], P('section', None, 'expert')
The draws below stay inside these ranges and needn't reach their ends.
Inputs may be any that keep to these rules, and one draw needn't show every extreme that they name: `routes`: in each layer and micro-batch the 64 rows of one device name one expert at most 3 times, and 3 is reached in every draw.
All inputs are finite; a program needn't handle non-finite values. No bound on the sum of `labels` on one device may be relied on, other than what follows from the above.
Results may differ from the reference program's by a relative error of at most 0.04.
Values may be sent and summed in bfloat16 or wider, within the bound.
No kernel may reach another device: no remote copies, remote signals or barrier semaphores. Data moves between devices by JAX's collectives and lax.ppermute only.
A program may use at most 128 MiB of HBM per device.

```python
import math
import jax
import jax.numpy as jnp
import numpy as np
from jax import lax

D = 2048
FE = 256
RANK = 128
MB = 2
ROWS = 64
EXPERTS = 32
ROWS_ALL = 2048
CAP = 3
N_SECTION = 8
N_EXPERT = 32


def with_ends(result, rng, low, high):
    index_at = [jax.random.randint(jax.random.fold_in(rng, axis), (), 0, length) for axis, length in enumerate(result.shape)]
    longest = result.shape.index(max(result.shape))
    next_to = index_at[:longest] + [(index_at[longest] + 1) % result.shape[longest]] + index_at[longest + 1:]
    return result.at[tuple(index_at)].set(low).at[tuple(next_to)].set(high)


def steps_of(key, dims, pieces, low, top_value):
    loudness, own = 1.0, jax.random.fold_in(key, 6)
    for position, blocks in pieces:
        heights = jnp.exp(jax.random.uniform(jax.random.fold_in(own, position), (blocks,), jnp.float32, low / len(pieces), top_value / len(pieces)))
        loudness = loudness * jnp.repeat(heights, dims[position] // blocks).reshape([-1 if axis == position else 1 for axis in range(len(dims))])
    return loudness


def deal_out(own_key, own, number, rows, amount, top, limit, slope):
    order = jax.random.permutation(own_key, amount)
    heavy_load, usual = portions_of(amount, rows * top, limit, slope, True), portions_of(amount, rows * top, limit, slope, False)
    places = jnp.arange(amount)

    def named(sizes, offset_by):
        used = int((sizes > 0).sum())
        fixed = max(1, used // 4)
        shifted = fixed + (places - fixed + offset_by * (used - fixed)) % max(1, amount - fixed)
        return jnp.zeros((amount,), jnp.int32).at[order[jnp.where(places < fixed, places, shifted)]].set(jnp.asarray(sizes, jnp.int32))

    sizes = jnp.where(number % 4 == 0, named(heavy_load, number // 4), named(usual, number - number // 4 - 1))
    mixed = jax.random.permutation(jax.random.fold_in(own, 3), amount)
    giver, taker = mixed[0:amount // 2 * 2:2], mixed[1:amount // 2 * 2:2]
    room = jnp.minimum(sizes[giver] - 1, limit - sizes[taker]) // 2
    room = jnp.where((giver == order[0]) | (taker == order[0]) | (sizes[taker] == 0), 0, jnp.maximum(room, 0))
    shifted = jax.random.randint(jax.random.fold_in(own, 4), (amount // 2,), 0, 1 << 20) % (room + 1)
    sizes = sizes.at[giver].add(-shifted).at[taker].add(shifted)
    items = jnp.searchsorted(jnp.cumsum(sizes), jnp.arange(rows * top), side="right").astype(jnp.int32)
    table = items.reshape(top, rows).T
    table = table[jax.random.permutation(jax.random.fold_in(own, 1), rows)]
    offset_by = jax.random.randint(jax.random.fold_in(own, 2), (rows, 1), 0, top)
    return jnp.take_along_axis(table, (jnp.arange(top)[None, :] + offset_by) % top, axis=1)


def portions_of(number_of, total, reach, lean, full):
    loads = [(1 << 20) // math.isqrt(standing ** lean) + 1 for standing in range(1, number_of + 1)]
    largest = reach if full else min(reach, max(-(-total // number_of), total * loads[0] // sum(loads)))
    least = 1 if total - largest >= number_of - 1 else 0
    holding, spare = [largest] + [least] * (number_of - 1), total - largest - least * (number_of - 1)
    while spare > 0:
        candidates = [i for i in range(1, number_of) if holding[i] < largest] or [i for i in range(1, number_of) if holding[i] < reach]
        whole, left = sum([loads[i] for i in candidates]), spare
        for i in candidates:
            more = min(reach - holding[i], max(1, left * loads[i] // whole), spare)
            holding[i] = holding[i] + more
            spare = spare - more
    return np.array(holding)


def scatter_about(key, extent, deviation, reach, split=(), held_as=jnp.bfloat16):
    result = deviation * jax.random.normal(key, extent, jnp.float32)
    if split:
        result = result * steps_of(key, extent, split, -0.22, 0.18)
    return jnp.clip(result, -reach, reach).astype(held_as)


def setup_inputs(seed: int = 0) -> dict:
    key_of = jax.random.split(jax.random.key(seed), 11)
    features = scatter_about(key_of[0], (MB, ROWS_ALL, D), 1.0, 6.0, ((1, 32),))
    labels = with_ends((jax.random.randint(key_of[1], (MB, ROWS_ALL), 0, 3) < 1).astype(jnp.int32), jax.random.fold_in(key_of[1], 1), 0, 1)
    routes_keys = jax.random.split(jax.random.fold_in(key_of[2], 1), N_SECTION * MB * ROWS_ALL // ROWS)
    routes_turns = jax.random.permutation(jax.random.fold_in(key_of[2], 3), N_SECTION * MB * ROWS_ALL // ROWS)
    routes = jax.vmap(lambda own, number: deal_out(jax.random.fold_in(key_of[2], 2), own, number, ROWS, EXPERTS, 1, CAP, 2))(routes_keys, routes_turns).reshape((N_SECTION, MB, ROWS_ALL, 1))
    route_gates = jnp.clip(0.25 + 0.75 * jax.random.uniform(key_of[3], (N_SECTION, MB, ROWS_ALL), jnp.float32) ** steps_of(key_of[3], (N_SECTION, MB, ROWS_ALL), ((0, 8), (2, 32)), -0.2, 0.2), 0.25, 1.0)
    gate_weight = scatter_about(key_of[4], (N_SECTION, EXPERTS, D, FE), D ** -0.5, 0.125, ((0, 8), (1, 32)))
    up_weight = scatter_about(key_of[5], (N_SECTION, EXPERTS, D, FE), D ** -0.5, 0.125, ((0, 8), (1, 32)))
    down_weight = scatter_about(key_of[6], (N_SECTION, EXPERTS, FE, D), FE ** -0.5, 0.375, ((0, 8), (1, 32)))
    lowrank_in = scatter_about(key_of[7], (N_SECTION, D, RANK), D ** -0.5, 0.125, ((0, 8),))
    lowrank_out = scatter_about(key_of[8], (N_SECTION, RANK, D), RANK ** -0.5, 0.5, ((0, 8),))
    head_weight = scatter_about(key_of[9], (D,), (D // 16) ** -0.5, 0.5, (), jnp.float32)
    return {"features": features, "labels": labels, "routes": routes, "route_gates": route_gates, "gate_weight": gate_weight, "up_weight": up_weight, "down_weight": down_weight, "lowrank_in": lowrank_in, "lowrank_out": lowrank_out, "head_weight": head_weight}


epsilon = 1e-06

def rms_scale(values):
    widened = values.astype(jnp.float32)
    return lax.rsqrt(lax.optimization_barrier(jnp.mean(widened * widened, axis=-1, keepdims=True)) + epsilon)

def norm_back(values, row_scale, grad_norm):
    widened = values.astype(jnp.float32)
    inner_mean = lax.optimization_barrier(jnp.mean(grad_norm * widened, axis=-1, keepdims=True))
    return row_scale * grad_norm - widened * (row_scale * row_scale * row_scale) * inner_mean

def expert_forward(slot_rows, gate_mat, up_mat, down_mat):
    gate_pre = jnp.dot(slot_rows, gate_mat, preferred_element_type=jnp.float32)
    up_pre = jnp.dot(slot_rows, up_mat, preferred_element_type=jnp.float32)
    hidden = (gate_pre * jax.nn.sigmoid(gate_pre) * up_pre).astype(jnp.bfloat16)
    return jnp.dot(hidden, down_mat, preferred_element_type=jnp.float32).astype(jnp.bfloat16)

def expert_backward(slot_rows, grad_out, gate_mat, up_mat, down_mat):
    gate_pre = jnp.dot(slot_rows, gate_mat, preferred_element_type=jnp.float32)
    up_pre = jnp.dot(slot_rows, up_mat, preferred_element_type=jnp.float32)
    gate_sig = jax.nn.sigmoid(gate_pre)
    gate_act = gate_pre * gate_sig
    hidden = (gate_act * up_pre).astype(jnp.bfloat16)
    grad_hidden = jnp.dot(grad_out, down_mat.T, preferred_element_type=jnp.float32)
    grad_gate = (grad_hidden * up_pre * (gate_sig * (1.0 + gate_pre * (1.0 - gate_sig)))).astype(jnp.bfloat16)
    grad_up = (grad_hidden * gate_act).astype(jnp.bfloat16)
    grad_slots = (jnp.dot(grad_gate, gate_mat.T, preferred_element_type=jnp.float32) + jnp.dot(grad_up, up_mat.T, preferred_element_type=jnp.float32)).astype(jnp.bfloat16)
    part_gate = jnp.dot(slot_rows.T, grad_gate, preferred_element_type=jnp.float32)
    part_up = jnp.dot(slot_rows.T, grad_up, preferred_element_type=jnp.float32)
    part_down = jnp.dot(hidden.T, grad_out, preferred_element_type=jnp.float32)
    return (grad_slots, part_gate, part_up, part_down)

def lowrank_parts(values, matrix_in):
    row_scale = rms_scale(values)
    normed = (values.astype(jnp.float32) * row_scale).astype(jnp.bfloat16)
    inner_pre = jnp.dot(normed, matrix_in, preferred_element_type=jnp.float32)
    inner_sig = jax.nn.sigmoid(inner_pre)
    inner_act = (inner_pre * inner_sig).astype(jnp.bfloat16)
    return (row_scale, normed, inner_pre, inner_sig, inner_act)

def lowrank_forward(values, matrix_in, matrix_out):
    row_scale, normed, inner_pre, inner_sig, inner_act = lowrank_parts(values, matrix_in)
    return (values.astype(jnp.float32) + jnp.dot(inner_act, matrix_out, preferred_element_type=jnp.float32)).astype(jnp.bfloat16)

def lowrank_backward(values, grad_rows, matrix_in, matrix_out):
    row_scale, normed, inner_pre, inner_sig, inner_act = lowrank_parts(values, matrix_in)
    grad_act = jnp.dot(grad_rows, matrix_out.T, preferred_element_type=jnp.float32)
    grad_pre = (grad_act * (inner_sig * (1.0 + inner_pre * (1.0 - inner_sig)))).astype(jnp.bfloat16)
    grad_norm = jnp.dot(grad_pre, matrix_in.T, preferred_element_type=jnp.float32)
    grad_input = (grad_rows.astype(jnp.float32) + norm_back(values, row_scale, grad_norm)).astype(jnp.bfloat16)
    part_in = jnp.dot(normed.T, grad_pre, preferred_element_type=jnp.float32)
    part_out = jnp.dot(inner_act.T, grad_rows, preferred_element_type=jnp.float32)
    return (grad_input, part_in, part_out)

def head_grad(values, targets, head_weight):
    row_scale = rms_scale(values)
    logits = row_scale[:, 0] * lax.optimization_barrier(jnp.sum(values.astype(jnp.float32) * head_weight[None, :], axis=1))
    grad_logit = jax.nn.sigmoid(logits) - targets.astype(jnp.float32)
    return norm_back(values, row_scale, grad_logit[:, None] * head_weight[None, :]).astype(jnp.bfloat16)

def slot_positions(expert_ids):
    chosen = (expert_ids[:, None] == jnp.arange(N_EXPERT, dtype=jnp.int32)[None, :]).astype(jnp.int32)
    ranking = jnp.cumsum(chosen, axis=0) - 1
    return lax.optimization_barrier(jnp.sum(chosen * ranking, axis=1)).astype(jnp.int32)

def moe_forward(values, expert_ids, gate_row, gate_mats, up_mats, down_mats, slot_limit):
    row_scale = rms_scale(values)
    normed = (values.astype(jnp.float32) * row_scale).astype(jnp.bfloat16)
    slot_index = slot_positions(expert_ids)
    buffer = jnp.zeros((N_EXPERT, slot_limit, values.shape[1]), jnp.bfloat16).at[expert_ids, slot_index].set(normed)
    served = lax.map(lambda packed: expert_forward(packed[0], packed[1], packed[2], packed[3]), (buffer, gate_mats, up_mats, down_mats))
    layer_out = values.astype(jnp.float32) + gate_row[:, None] * served[expert_ids, slot_index].astype(jnp.float32)
    return layer_out.astype(jnp.bfloat16)

def moe_backward(values, grad_rows, expert_ids, gate_row, gate_mats, up_mats, down_mats, slot_limit):
    row_scale = rms_scale(values)
    normed = (values.astype(jnp.float32) * row_scale).astype(jnp.bfloat16)
    slot_index = slot_positions(expert_ids)
    grad_out = (gate_row[:, None] * grad_rows.astype(jnp.float32)).astype(jnp.bfloat16)
    empty = jnp.zeros((N_EXPERT, slot_limit, values.shape[1]), jnp.bfloat16)
    slot_rows = empty.at[expert_ids, slot_index].set(normed)
    slot_grads = empty.at[expert_ids, slot_index].set(grad_out)
    grad_slots, part_gate, part_up, part_down = lax.map(lambda packed: expert_backward(packed[0], packed[1], packed[2], packed[3], packed[4]), (slot_rows, slot_grads, gate_mats, up_mats, down_mats))
    grad_norm = grad_slots[expert_ids, slot_index].astype(jnp.float32)
    grad_input = (grad_rows.astype(jnp.float32) + norm_back(values, row_scale, grad_norm)).astype(jnp.bfloat16)
    return (grad_input, part_gate, part_up, part_down)

def reference(features, labels, routes, route_gates, gate_weight, up_weight, down_weight, lowrank_in, lowrank_out, head_weight):
    feature_width = features.shape[-1]
    slot_limit = MB * N_EXPERT * CAP
    hidden_rows = features.reshape(-1, feature_width)
    moe_inputs = []
    for layer_id in range(N_SECTION):
        moe_inputs.append(hidden_rows)
        hidden_rows = moe_forward(hidden_rows, routes[layer_id].reshape(-1), route_gates[layer_id].reshape(-1), gate_weight[layer_id], up_weight[layer_id], down_weight[layer_id], slot_limit)
    low_inputs = [None] * N_SECTION
    for layer_id in reversed(range(N_SECTION)):
        low_inputs[layer_id] = hidden_rows
        hidden_rows = lowrank_forward(hidden_rows, lowrank_in[layer_id], lowrank_out[layer_id])
    grad_rows = head_grad(hidden_rows, labels.reshape(-1), head_weight)
    grads_in = [None] * N_SECTION
    grads_out = [None] * N_SECTION
    for layer_id in range(N_SECTION):
        grad_rows, part_in, part_out = lowrank_backward(low_inputs[layer_id], grad_rows, lowrank_in[layer_id], lowrank_out[layer_id])
        grads_in[layer_id] = part_in
        grads_out[layer_id] = part_out
    grads_gate = [None] * N_SECTION
    grads_up = [None] * N_SECTION
    grads_down = [None] * N_SECTION
    for layer_id in reversed(range(N_SECTION)):
        grad_rows, part_gate, part_up, part_down = moe_backward(moe_inputs[layer_id], grad_rows, routes[layer_id].reshape(-1), route_gates[layer_id].reshape(-1), gate_weight[layer_id], up_weight[layer_id], down_weight[layer_id], slot_limit)
        grads_gate[layer_id] = part_gate
        grads_up[layer_id] = part_up
        grads_down[layer_id] = part_down
    return (jnp.stack(grads_gate), jnp.stack(grads_up), jnp.stack(grads_down), jnp.stack(grads_in), jnp.stack(grads_out))
```

```python
import jax
import jax.numpy as jnp
from jax import lax
from jax.sharding import PartitionSpec as P

epsilon = 1e-06
capacity = 3


def dot(left, right):
    return jnp.dot(left, right, preferred_element_type=jnp.float32)


def dot_t(left, right):
    return lax.dot_general(left, right, (((1,), (1,)), ((), ())), preferred_element_type=jnp.float32)


def dot_tn(left, right):
    return lax.dot_general(left, right, (((0,), (0,)), ((), ())), preferred_element_type=jnp.float32)


def rms_scale(values):
    widened = values.astype(jnp.float32)
    return lax.rsqrt(jnp.mean(widened * widened, axis=-1, keepdims=True) + epsilon)


def norm_back(values, row_scale, grad_norm):
    widened = values.astype(jnp.float32)
    inner_mean = jnp.mean(grad_norm * widened, axis=-1, keepdims=True)
    return row_scale * grad_norm - widened * (row_scale * row_scale * row_scale) * inner_mean


def lowrank_parts(values, matrix_in):
    row_scale = rms_scale(values)
    normed = (values.astype(jnp.float32) * row_scale).astype(jnp.bfloat16)
    inner_pre = dot(normed, matrix_in)
    inner_sig = jax.nn.sigmoid(inner_pre)
    inner_act = (inner_pre * inner_sig).astype(jnp.bfloat16)
    return (row_scale, normed, inner_pre, inner_sig, inner_act)


def lowrank_forward(values, matrix_in, matrix_out):
    inner_act = lowrank_parts(values, matrix_in)[4]
    return (values.astype(jnp.float32) + dot(inner_act, matrix_out)).astype(jnp.bfloat16)


def lowrank_backward(values, grad_rows, matrix_in, matrix_out):
    row_scale, normed, inner_pre, inner_sig, inner_act = lowrank_parts(values, matrix_in)
    grad_act = dot_t(grad_rows, matrix_out)
    grad_pre = (grad_act * (inner_sig * (1.0 + inner_pre * (1.0 - inner_sig)))).astype(jnp.bfloat16)
    grad_norm = dot_t(grad_pre, matrix_in)
    grad_input = (grad_rows.astype(jnp.float32) + norm_back(values, row_scale, grad_norm)).astype(
        jnp.bfloat16
    )
    return (grad_input, dot_tn(normed, grad_pre), dot_tn(inner_act, grad_rows))


def head_grad(values, targets, head_weight):
    row_scale = rms_scale(values)
    logits = row_scale[:, 0] * jnp.sum(values.astype(jnp.float32) * head_weight[None, :], axis=1)
    grad_logit = jax.nn.sigmoid(logits) - targets.astype(jnp.float32)
    return norm_back(values, row_scale, grad_logit[:, None] * head_weight[None, :]).astype(
        jnp.bfloat16
    )


def slot_of_rows(expert_ids, expert_count, stride, offset):
    chosen = (expert_ids[:, None] == jnp.arange(expert_count, dtype=jnp.int32)[None, :]).astype(
        jnp.int32
    )
    earlier = jnp.arange(expert_ids.shape[0])[:, None] > jnp.arange(expert_ids.shape[0])[None, :]
    same = expert_ids[:, None] == expert_ids[None, :]
    rank = jnp.sum((same & earlier).astype(jnp.int32), axis=1)
    return expert_ids * stride + offset + rank


def table_of(slots, slot_count):
    grid = jnp.arange(slot_count, dtype=jnp.int32)
    return (grid[:, None] == slots[None, :]).astype(jnp.bfloat16)


def exchange(buffer, expert_count):
    shaped = buffer.reshape(expert_count, -1, buffer.shape[1])
    moved = lax.all_to_all(shaped, "expert", split_axis=0, concat_axis=0, tiled=True)
    return moved.reshape(buffer.shape)


def expert_forward(values, table, gate_row, mats):
    gate_mat, up_mat, down_mat = mats
    expert_count = lax.axis_size("expert")
    row_scale = rms_scale(values)
    normed = (values.astype(jnp.float32) * row_scale).astype(jnp.bfloat16)
    kept = exchange(dot(table, normed).astype(jnp.bfloat16), expert_count)
    gate_pre = dot(kept, gate_mat)
    up_pre = dot(kept, up_mat)
    hidden = (gate_pre * jax.nn.sigmoid(gate_pre) * up_pre).astype(jnp.bfloat16)
    served = dot(hidden, down_mat).astype(jnp.bfloat16)
    returned = exchange(served, expert_count)
    layer_out = values.astype(jnp.float32) + gate_row[:, None] * dot_tn(table, returned)
    return (layer_out.astype(jnp.bfloat16), kept)


def expert_backward(values, grad_rows, table, gate_row, kept, mats):
    gate_mat, up_mat, down_mat = mats
    expert_count = lax.axis_size("expert")
    grad_out = (gate_row[:, None] * grad_rows.astype(jnp.float32)).astype(jnp.bfloat16)
    slot_grads = exchange(dot(table, grad_out).astype(jnp.bfloat16), expert_count)
    gate_pre = dot(kept, gate_mat)
    up_pre = dot(kept, up_mat)
    gate_sig = jax.nn.sigmoid(gate_pre)
    gate_act = gate_pre * gate_sig
    hidden = (gate_act * up_pre).astype(jnp.bfloat16)
    grad_hidden = dot_t(slot_grads, down_mat)
    grad_gate = (grad_hidden * up_pre * (gate_sig * (1.0 + gate_pre * (1.0 - gate_sig)))).astype(
        jnp.bfloat16
    )
    grad_up = (grad_hidden * gate_act).astype(jnp.bfloat16)
    grad_slots = (dot_t(grad_gate, gate_mat) + dot_t(grad_up, up_mat)).astype(jnp.bfloat16)
    returned = exchange(grad_slots, expert_count)
    grad_norm = dot_tn(table, returned)
    row_scale = rms_scale(values)
    grad_input = (grad_rows.astype(jnp.float32) + norm_back(values, row_scale, grad_norm)).astype(
        jnp.bfloat16
    )
    wide = jnp.concatenate([kept, slot_grads], axis=1)
    narrow = jnp.concatenate([hidden, grad_gate, grad_up], axis=1)
    return (grad_input, (wide, narrow))


def local(
    features,
    labels,
    routes,
    route_gates,
    gate_weight,
    up_weight,
    down_weight,
    lowrank_in,
    lowrank_out,
    head_weight,
):
    section_count = lax.axis_size("section")
    section = lax.axis_index("section")
    expert_count = lax.axis_size("expert")
    micro_count, row_count, width = features.shape
    inner = gate_weight.shape[3]
    parity = section % 2
    is_even = parity == 0
    pair = section // 2
    partners = [(s, s ^ 1) for s in range(section_count)]

    def swap(value):
        return lax.ppermute(value, "section", partners)

    def ring(value, steps):
        return lax.ppermute(
            value, "section", [(s, (s + steps) % section_count) for s in range(section_count)]
        )

    own = (gate_weight[0, 0], up_weight[0, 0], down_weight[0, 0])
    other = tuple(swap(mat) for mat in own)
    mats_even = tuple(jnp.where(is_even, a, b) for a, b in zip(own, other))
    mats_odd = tuple(jnp.where(is_even, b, a) for a, b in zip(own, other))

    ids = routes[0, :, :, 0]
    plan = jnp.concatenate([ids.astype(jnp.float32), route_gates[0]], axis=0)
    plan_other = swap(plan)

    def pick(first, second):
        chosen = jnp.where(is_even, first, second)
        mine = jnp.where(is_even, chosen[0::2], chosen[1::2])
        slots = slot_of_rows(mine[0].astype(jnp.int32), expert_count, capacity, 0)
        return (table_of(slots, expert_count * capacity), mine[1])

    table_even, gate_even = pick(plan, plan_other)
    table_odd, gate_odd = pick(plan_other, plan)
    joint_slots = jnp.concatenate(
        [
            slot_of_rows(ids[m], expert_count, capacity * micro_count, capacity * m)
            for m in range(micro_count)
        ]
    )
    table_all = table_of(joint_slots, expert_count * capacity * micro_count)
    gate_all = route_gates[0].reshape(-1)

    first_rows = features.reshape(-1, width)
    second_rows, kept_all = expert_forward(first_rows, table_all, gate_all, own)
    crossing = swap(second_rows[row_count:])
    rows = jnp.where(is_even, second_rows[:row_count], crossing)

    layer_rows = {}
    layer_kept = {}
    for layer in range(1, section_count):
        odd = layer % 2 == 1
        layer_rows[layer] = rows
        rows, layer_kept[layer] = expert_forward(
            rows,
            table_odd if odd else table_even,
            gate_odd if odd else gate_even,
            mats_odd if odd else mats_even,
        )
        if layer == 2:
            low_in, low_out, rows = lax.optimization_barrier((lowrank_in[0], lowrank_out[0], rows))
            all_in = lax.all_gather(low_in, "section")
            all_out = lax.all_gather(low_out, "section")
        if odd and layer < section_count - 1:
            rows = ring(rows, 2)

    low_rows = {}
    for index in reversed(range(section_count)):
        low_rows[index] = rows
        rows = lowrank_forward(rows, all_in[index], all_out[index])
    grads = head_grad(rows, jnp.where(is_even, labels[0], labels[1]), head_weight)
    parts_in = []
    parts_out = []
    for index in range(section_count):
        grads, part_in, part_out = lowrank_backward(
            low_rows[index], grads, all_in[index], all_out[index]
        )
        parts_in.append(part_in.astype(jnp.bfloat16))
        parts_out.append(part_out.astype(jnp.bfloat16))
    valid = pair == section_count // 2 - 1

    def spread_sum(parts, dimension):
        stacked = jnp.stack(parts)
        stacked = jnp.where(valid, stacked, jnp.zeros_like(stacked))
        mine = lax.psum_scatter(stacked, "section", scatter_dimension=0, tiled=False)
        return lax.psum_scatter(mine, "expert", scatter_dimension=dimension, tiled=True).astype(
            jnp.float32
        )

    share_in = spread_sum(parts_in, 0)
    share_out = spread_sum(parts_out, 1)

    saved = {0: None, 1: None}
    for layer in reversed(range(1, section_count)):
        odd = layer % 2 == 1
        grads, record = expert_backward(
            layer_rows[layer],
            grads,
            table_odd if odd else table_even,
            gate_odd if odd else gate_even,
            layer_kept[layer],
            mats_odd if odd else mats_even,
        )
        here = pair == layer // 2
        past = saved[layer % 2]
        saved[layer % 2] = (
            record
            if past is None
            else tuple(jnp.where(here, new, old) for new, old in zip(record, past))
        )
        if not odd:
            grads = ring(grads, -2)

    crossing = swap(grads)
    all_grads = jnp.concatenate([grads, crossing], axis=0)
    sent = tuple(swap(jnp.where(is_even, b, a)) for a, b in zip(saved[0], saved[1]))
    held = tuple(jnp.where(is_even, a, b) for a, b in zip(saved[0], saved[1]))
    _, record = expert_backward(first_rows, all_grads, table_all, gate_all, kept_all, own)
    final_wide, final_narrow = (
        jnp.where(section == 0, joint, jnp.concatenate([mine, theirs], axis=0))
        for joint, mine, theirs in zip(record, held, sent)
    )
    kept, slot_grads = (final_wide[:, :width], final_wide[:, width:])
    hidden, grad_gate, grad_up = (final_narrow[:, inner * k : inner * (k + 1)] for k in range(3))
    return (
        dot_tn(kept, grad_gate)[None, None],
        dot_tn(kept, grad_up)[None, None],
        dot_tn(hidden, slot_grads)[None, None],
        share_in[None],
        share_out[None],
    )


def solution(mesh):
    return jax.shard_map(
        local,
        mesh=mesh,
        in_specs=(
            P(None, "expert", None),
            P(None, "expert"),
            P("section", None, "expert", None),
            P("section", None, "expert"),
            P("section", "expert", None, None),
            P("section", "expert", None, None),
            P("section", "expert", None, None),
            P("section", None, None),
            P("section", None, None),
            P(),
        ),
        out_specs=(
            P("section", "expert", None, None),
            P("section", "expert", None, None),
            P("section", "expert", None, None),
            P("section", "expert", None),
            P("section", None, "expert"),
        ),
        check_vma=False,
    )
```

```python
import jax
import jax.numpy as jnp
from jax import lax
from jax.experimental import pallas as pl
from jax.experimental.pallas import tpu as pltpu
from jax.sharding import PartitionSpec as P

epsilon = 1e-06
capacity = 3


def dot(left, right):
    return jnp.dot(left, right, preferred_element_type=jnp.float32)


def dot_t(left, right):
    return lax.dot_general(left, right, (((1,), (1,)), ((), ())), preferred_element_type=jnp.float32)


def dot_tn(left, right):
    return lax.dot_general(left, right, (((0,), (0,)), ((), ())), preferred_element_type=jnp.float32)


def rms_scale(values):
    widened = values.astype(jnp.float32)
    return lax.rsqrt(jnp.mean(widened * widened, axis=-1, keepdims=True) + epsilon)


def norm_back(values, row_scale, grad_norm):
    widened = values.astype(jnp.float32)
    inner_mean = jnp.mean(grad_norm * widened, axis=-1, keepdims=True)
    return row_scale * grad_norm - widened * (row_scale * row_scale * row_scale) * inner_mean


def slot_of_rows(expert_ids, expert_count, stride, offset):
    chosen = (expert_ids[:, None] == jnp.arange(expert_count, dtype=jnp.int32)[None, :]).astype(
        jnp.int32
    )
    earlier = jnp.arange(expert_ids.shape[0])[:, None] > jnp.arange(expert_ids.shape[0])[None, :]
    same = expert_ids[:, None] == expert_ids[None, :]
    rank = jnp.sum((same & earlier).astype(jnp.int32), axis=1)
    return expert_ids * stride + offset + rank


def table_of(slots, slot_count):
    grid = jnp.arange(slot_count, dtype=jnp.int32)
    return (grid[:, None] == slots[None, :]).astype(jnp.bfloat16)


def run_kernel(body, out_shape, scratch, *operands):
    return pl.pallas_call(
        body,
        out_shape=out_shape,
        in_specs=[pl.BlockSpec(memory_space=pltpu.VMEM) for _ in operands],
        out_specs=jax.tree.map(lambda _: pl.BlockSpec(memory_space=pltpu.VMEM), out_shape),
        scratch_shapes=scratch,
        compiler_params=pltpu.CompilerParams(vmem_limit_bytes=40 * 1024 * 1024),
    )(*operands)


def array(shape, dtype=jnp.bfloat16):
    return jax.ShapeDtypeStruct(shape, dtype)


def unpack_slots(source, rows):
    count, depth, _ = source.shape
    for index in range(count):
        rows[depth * index : depth * (index + 1), :] = source[index].astype(jnp.float32)


def pack_slots(rows, target):
    count, depth, _ = target.shape
    for index in range(count):
        target[index] = rows[depth * index : depth * (index + 1), :].astype(jnp.bfloat16)


def normed_rows(values):
    widened = values.astype(jnp.float32)
    return (widened * rms_scale(values)).astype(jnp.bfloat16)


def send_body(values, table, target, rows):
    rows[...] = dot(table[...], normed_rows(values[...]))
    pack_slots(rows, target)


def take_body(returned, pick_table, values, gate, result, rows):
    unpack_slots(returned, rows)
    gathered = dot(pick_table[...], rows[...].astype(jnp.bfloat16))
    result[...] = (values[...].astype(jnp.float32) + gate[...] * gathered).astype(jnp.bfloat16)


def turn_body(returned, pick_table, values, gate, table, result, target, rows):
    take_body(returned, pick_table, values, gate, result, rows)
    send_body(result, table, target, rows)


def send_back_body(grads, gate, table, target, rows):
    grad_out = (gate[...] * grads[...].astype(jnp.float32)).astype(jnp.bfloat16)
    rows[...] = dot(table[...], grad_out)
    pack_slots(rows, target)


def take_back_body(returned, pick_table, values, grads, result, rows):
    unpack_slots(returned, rows)
    grad_norm = dot(pick_table[...], rows[...].astype(jnp.bfloat16))
    value = values[...]
    result[...] = (
        grads[...].astype(jnp.float32) + norm_back(value, rms_scale(value), grad_norm)
    ).astype(jnp.bfloat16)


def turn_back_body(returned, pick_table, values, grads, gate, table, result, target, rows):
    take_back_body(returned, pick_table, values, grads, result, rows)
    send_back_body(result, gate, table, target, rows)


def serve_body(received, gate_mat, up_mat, down_mat, served, kept, gate_pre, up_pre, rows):
    unpack_slots(received, rows)
    kept[...] = rows[...].astype(jnp.bfloat16)
    gate_pre[...] = dot(kept[...], gate_mat[...])
    up_pre[...] = dot(kept[...], up_mat[...])
    gate = gate_pre[...]
    hidden = (gate * jax.nn.sigmoid(gate) * up_pre[...]).astype(jnp.bfloat16)
    rows[...] = dot(hidden, down_mat[...])
    pack_slots(rows, served)


def serve_back_rows(received, gate_pre, up_pre, down_mat, slot_grads, narrow, rows):
    unpack_slots(received, rows)
    slot_grads[...] = rows[...].astype(jnp.bfloat16)
    gate = gate_pre[...]
    up = up_pre[...]
    gate_sig = jax.nn.sigmoid(gate)
    gate_act = gate * gate_sig
    grad_hidden = dot_t(slot_grads[...], down_mat[...])
    grad_gate = (grad_hidden * up * (gate_sig * (1.0 + gate * (1.0 - gate_sig)))).astype(
        jnp.bfloat16
    )
    grad_up = (grad_hidden * gate_act).astype(jnp.bfloat16)
    inner = gate.shape[1]
    narrow[:, :inner] = (gate_act * up).astype(jnp.bfloat16)
    narrow[:, inner : 2 * inner] = grad_gate
    narrow[:, 2 * inner :] = grad_up
    return (grad_gate, grad_up)


def serve_back_body(
    received, gate_pre, up_pre, gate_mat, up_mat, down_mat, target, slot_grads, narrow, rows
):
    grad_gate, grad_up = serve_back_rows(
        received, gate_pre, up_pre, down_mat, slot_grads, narrow, rows
    )
    rows[...] = dot_t(grad_gate, gate_mat[...]) + dot_t(grad_up, up_mat[...])
    pack_slots(rows, target)


def lowrank_body(
    rows, mats, targets, head, grads, all_normed, all_act, all_pre, all_grads, values, inner, scale
):
    count = mats.shape[0]
    values[0] = rows[...]

    def forward(step, carry):
        index = count - 1 - step
        value = values[step]
        row_scale = rms_scale(value)
        normed = (value.astype(jnp.float32) * row_scale).astype(jnp.bfloat16)
        inner_pre = dot(normed, mats[index, 0])
        act = (inner_pre * jax.nn.sigmoid(inner_pre)).astype(jnp.bfloat16)
        all_normed[index] = normed
        all_act[index] = act
        inner[index] = inner_pre
        scale[index] = row_scale
        values[step + 1] = (
            value.astype(jnp.float32) + dot_t(act, mats[index, 1])
        ).astype(jnp.bfloat16)
        return carry

    lax.fori_loop(0, count, forward, 0)
    final = values[count]
    row_scale = rms_scale(final)
    logits = row_scale * jnp.sum(final.astype(jnp.float32) * head[...], axis=1, keepdims=True)
    grad_logit = jax.nn.sigmoid(logits) - targets[...]
    grads[...] = norm_back(final, row_scale, grad_logit * head[...]).astype(jnp.bfloat16)

    def backward(index, carry):
        value = values[count - 1 - index]
        grad = grads[...]
        inner_pre = inner[index]
        inner_sig = jax.nn.sigmoid(inner_pre)
        grad_act = dot(grad, mats[index, 1])
        grad_pre = (grad_act * (inner_sig * (1.0 + inner_pre * (1.0 - inner_sig)))).astype(
            jnp.bfloat16
        )
        grad_norm = dot_t(grad_pre, mats[index, 0])
        all_pre[index] = grad_pre
        all_grads[index] = grad
        grads[...] = (
            grad.astype(jnp.float32) + norm_back(value, scale[index], grad_norm)
        ).astype(jnp.bfloat16)
        return carry

    lax.fori_loop(0, count, backward, 0)


def lowrank_layers(rows, mats, targets, head):
    count, rank = (mats.shape[0], mats.shape[3])
    row_count, width = rows.shape
    wide = array((count, row_count, width))
    narrow = array((count, row_count, rank))
    return run_kernel(
        lowrank_body,
        (array(rows.shape), wide, narrow, narrow, wide),
        [
            pltpu.VMEM((count + 1, row_count, width), jnp.bfloat16),
            pltpu.VMEM((count, row_count, rank), jnp.float32),
            pltpu.VMEM((count, row_count, 1), jnp.float32),
        ],
        rows,
        mats,
        targets,
        head,
    )


def exchange(buffer):
    return lax.all_to_all(buffer, "expert", split_axis=0, concat_axis=0, tiled=True)


def work_rows(slots, width):
    return [pltpu.VMEM((slots, width), jnp.float32)]


def packed_shape(table, width):
    count = lax.axis_size("expert")
    return array((count, table.shape[0] // count, width))


def send(values, table):
    width = values.shape[1]
    return run_kernel(
        send_body, packed_shape(table, width), work_rows(table.shape[0], width), values, table
    )


def take(returned, route, values):
    table, pick_table, gate = route
    width = values.shape[1]
    return run_kernel(
        take_body,
        array(values.shape),
        work_rows(table.shape[0], width),
        returned,
        pick_table,
        values,
        gate,
    )


def turn(returned, route, values, next_table):
    table, pick_table, gate = route
    width = values.shape[1]
    return run_kernel(
        turn_body,
        (array(values.shape), packed_shape(next_table, width)),
        work_rows(table.shape[0], width),
        returned,
        pick_table,
        values,
        gate,
        next_table,
    )


def send_back(grads, route):
    table, _, gate = route
    width = grads.shape[1]
    return run_kernel(
        send_back_body,
        packed_shape(table, width),
        work_rows(table.shape[0], width),
        grads,
        gate,
        table,
    )


def take_back(returned, route, values, grads):
    table, pick_table, _ = route
    width = values.shape[1]
    return run_kernel(
        take_back_body,
        array(values.shape),
        work_rows(table.shape[0], width),
        returned,
        pick_table,
        values,
        grads,
    )


def turn_back(returned, route, values, grads, next_route):
    table, pick_table, _ = route
    width = values.shape[1]
    return run_kernel(
        turn_back_body,
        (array(values.shape), packed_shape(next_route[0], width)),
        work_rows(table.shape[0], width),
        returned,
        pick_table,
        values,
        grads,
        next_route[2],
        next_route[0],
    )


def serve(received, mats):
    count, depth, width = received.shape
    slots, inner = (count * depth, mats[0].shape[1])
    return run_kernel(
        serve_body,
        (
            array(received.shape),
            array((slots, width)),
            array((slots, inner), jnp.float32),
            array((slots, inner), jnp.float32),
        ),
        work_rows(slots, width),
        received,
        *mats,
    )


def serve_back(received, gate_pre, up_pre, mats):
    count, depth, width = received.shape
    slots, inner = gate_pre.shape
    return run_kernel(
        serve_back_body,
        (array(received.shape), array((slots, width)), array((slots, 3 * inner))),
        work_rows(slots, width),
        received,
        gate_pre,
        up_pre,
        *mats,
    )


def serve_last(received, gate_pre, up_pre, down_mat):
    count, depth, width = received.shape
    slots, inner = gate_pre.shape
    return run_kernel(
        lambda *refs: serve_back_rows(*refs) and None,
        (array((slots, width)), array((slots, 3 * inner))),
        work_rows(slots, width),
        received,
        gate_pre,
        up_pre,
        down_mat,
    )


def local(
    features,
    labels,
    routes,
    route_gates,
    gate_weight,
    up_weight,
    down_weight,
    lowrank_in,
    lowrank_out,
    head_weight,
):
    section_count = lax.axis_size("section")
    section = lax.axis_index("section")
    expert_count = lax.axis_size("expert")
    micro_count, row_count, width = features.shape
    inner = gate_weight.shape[3]
    is_even = section % 2 == 0
    pair = section // 2
    to_odd = [(s, s + 1) for s in range(0, section_count, 2)]
    to_even = [(s + 1, s) for s in range(0, section_count, 2)]

    def swap(value):
        return lax.ppermute(value, "section", to_odd + to_even)

    def hop(value, layer):
        first = 0 if layer % 4 < 2 else 2
        links = []
        for start in range(first, first + section_count, 4):
            for lower in (start, start + 1):
                low_end, high_end = (lower % section_count, (lower + 2) % section_count)
                links += [(low_end, high_end), (high_end, low_end)]
        half = value.shape[0] // 2
        parts = [lax.ppermute(part, "section", links) for part in (value[:half], value[half:])]
        return jnp.concatenate(parts, axis=0)

    own = (gate_weight[0, 0], up_weight[0, 0], down_weight[0, 0])
    other = (swap(own[0]), swap(own[1]))
    down_back = lax.ppermute(own[2], "section", to_even)
    mats_odd = tuple(jnp.where(is_even, b, a) for a, b in zip(own, other + (down_back,)))

    ids = routes[0, :, :, 0]
    plan = jnp.concatenate([ids.astype(jnp.float32), route_gates[0]], axis=0)
    plan_other = swap(plan)

    def route_of(slots, slot_count, gates):
        table = table_of(slots, slot_count)
        grid = jnp.arange(slot_count, dtype=jnp.int32)
        pick_table = (slots[:, None] == grid[None, :]).astype(jnp.bfloat16)
        return (table, pick_table, gates[:, None])

    def pick(first, second):
        chosen = jnp.where(is_even, first, second)
        mine = jnp.where(is_even, chosen[0::2], chosen[1::2])
        slots = slot_of_rows(mine[0].astype(jnp.int32), expert_count, capacity, 0)
        return route_of(slots, expert_count * capacity, mine[1])

    route_even = pick(plan, plan_other)
    route_odd = pick(plan_other, plan)
    joint_slots = jnp.concatenate(
        [
            slot_of_rows(ids[m], expert_count, capacity * micro_count, capacity * m)
            for m in range(micro_count)
        ]
    )
    route_all = route_of(
        joint_slots, expert_count * capacity * micro_count, route_gates[0].reshape(-1)
    )
    routing = [route_odd if layer % 2 else route_even for layer in range(section_count)]

    first_rows = features.reshape(-1, width)
    served, kept_all, gate_all, up_all = serve(exchange(send(first_rows, route_all[0])), own)
    second_rows = take(exchange(served), route_all, first_rows)
    crossing = lax.ppermute(second_rows[row_count:], "section", to_odd)
    rows = jnp.where(is_even, second_rows[:row_count], crossing)
    rows, late = lax.optimization_barrier((rows, own[2]))
    down_on = lax.ppermute(late, "section", to_odd)
    mats_even = tuple(jnp.where(is_even, a, b) for a, b in zip(own, other + (down_on,)))
    mats = [mats_odd if layer % 2 else mats_even for layer in range(section_count)]

    layer_rows = {}
    layer_kept = {}
    sending = send(rows, routing[1][0])
    for layer in range(1, section_count):
        layer_rows[layer] = rows
        served, *layer_kept[layer] = serve(exchange(sending), mats[layer])
        returned = exchange(served)
        if layer % 2 == 0:
            rows, sending = turn(returned, routing[layer], rows, routing[layer + 1][0])
            if layer == 2:
                low_own = jnp.stack([lowrank_in[0], lowrank_out[0].T])
                low_own, rows = lax.optimization_barrier((low_own, rows))
                low_mats = lax.all_gather(low_own, "section")
        else:
            rows = take(returned, routing[layer], rows)
            if layer < section_count - 1:
                rows = hop(rows, layer)
                sending = send(rows, routing[layer + 1][0])

    targets = jnp.where(is_even, labels[0], labels[1]).astype(jnp.float32)[:, None]
    grads, low_normed, low_act, low_pre, low_grads = lowrank_layers(
        rows, low_mats, targets, head_weight[None, :]
    )

    def low_part(wide, narrow):
        part = dot_tn(wide, narrow).astype(jnp.bfloat16)
        return part.reshape(expert_count, 1, -1, part.shape[1])

    parts = jnp.stack(
        [
            jnp.concatenate(
                [
                    low_part(low_normed[index], low_pre[index]),
                    low_part(low_grads[index], low_act[index]),
                ],
                axis=1,
            )
            for index in range(section_count)
        ],
        axis=1,
    )
    last_pair = section_count // 2 - 1
    parts = jnp.where(pair == last_pair, parts, jnp.zeros_like(parts))

    saved = {0: None, 1: None}
    sending = send_back(grads, routing[section_count - 1])
    for layer in reversed(range(1, section_count)):
        kept, gate_pre, up_pre = layer_kept[layer]
        target, slot_grads, narrow = serve_back(exchange(sending), gate_pre, up_pre, mats[layer])
        returned = exchange(target)
        values = layer_rows[layer]
        if layer % 2 == 1 and layer > 1:
            grads, sending = turn_back(returned, routing[layer], values, grads, routing[layer - 1])
        else:
            grads = take_back(returned, routing[layer], values, grads)
        record = (kept, slot_grads, narrow)
        past = saved[layer % 2]
        saved[layer % 2] = (
            record
            if past is None
            else tuple(
                jnp.where(pair == layer // 2, new, old) for new, old in zip(record, past)
            )
        )
        if layer == 6:
            parts, grads = lax.optimization_barrier((parts, grads))
            share = lax.psum_scatter(
                parts.reshape(-1, parts.shape[-1]), "expert", scatter_dimension=0, tiled=True
            ).reshape(parts.shape[1:])
        if layer == 2:
            share, grads = lax.optimization_barrier((share, grads))
            share = lax.all_to_all(share, "section", split_axis=0, concat_axis=0, tiled=True)
        if layer % 2 == 0:
            grads = hop(grads, layer - 2)
            sending = send_back(grads, routing[layer - 1])

    all_grads = jnp.concatenate([grads, lax.ppermute(grads, "section", to_even)], axis=0)
    theirs = tuple(swap(jnp.where(is_even, b, a)) for a, b in zip(saved[0], saved[1]))
    held = tuple(jnp.where(is_even, a, b) for a, b in zip(saved[0], saved[1]))
    joint = (kept_all,) + tuple(
        serve_last(exchange(send_back(all_grads, route_all)), gate_all, up_all, own[2])
    )
    kept, slot_grads, narrow = (
        jnp.where(section == 0, both, jnp.concatenate([mine, other], axis=0))
        for both, mine, other in zip(joint, held, theirs)
    )
    hidden, grad_gate, grad_up = (narrow[:, inner * k : inner * (k + 1)] for k in range(3))
    share = jnp.sum(share[2 * last_pair :].astype(jnp.float32), axis=0)
    return (
        dot_tn(kept, grad_gate)[None, None],
        dot_tn(kept, grad_up)[None, None],
        dot_tn(hidden, slot_grads)[None, None],
        share[0][None],
        share[1].T[None],
    )


def solution(mesh):
    return jax.shard_map(
        local,
        mesh=mesh,
        in_specs=(
            P(None, "expert", None),
            P(None, "expert"),
            P("section", None, "expert", None),
            P("section", None, "expert"),
            P("section", "expert", None, None),
            P("section", "expert", None, None),
            P("section", "expert", None, None),
            P("section", None, None),
            P("section", None, None),
            P(),
        ),
        out_specs=(
            P("section", "expert", None, None),
            P("section", "expert", None, None),
            P("section", "expert", None, None),
            P("section", "expert", None),
            P("section", None, "expert"),
        ),
        check_vma=False,
    )
```

```python
import jax
import jax.numpy as jnp
from jax import lax
from jax.experimental import pallas as pl
from jax.experimental.pallas import tpu as pltpu
from jax.sharding import PartitionSpec as P

epsilon = 1e-06
capacity = 3


def dot(left, right):
    return jnp.dot(left, right, preferred_element_type=jnp.float32)


def dot_t(left, right):
    return lax.dot_general(left, right, (((1,), (1,)), ((), ())), preferred_element_type=jnp.float32)


def dot_tn(left, right):
    return lax.dot_general(left, right, (((0,), (0,)), ((), ())), preferred_element_type=jnp.float32)


def rms_scale(values):
    widened = values.astype(jnp.float32)
    return lax.rsqrt(jnp.mean(widened * widened, axis=-1, keepdims=True) + epsilon)


def norm_back(values, row_scale, grad_norm):
    widened = values.astype(jnp.float32)
    inner_mean = jnp.mean(grad_norm * widened, axis=-1, keepdims=True)
    return row_scale * grad_norm - widened * (row_scale * row_scale * row_scale) * inner_mean


def slot_of_rows(expert_ids, expert_count, stride, offset):
    chosen = (expert_ids[:, None] == jnp.arange(expert_count, dtype=jnp.int32)[None, :]).astype(
        jnp.int32
    )
    earlier = jnp.arange(expert_ids.shape[0])[:, None] > jnp.arange(expert_ids.shape[0])[None, :]
    same = expert_ids[:, None] == expert_ids[None, :]
    rank = jnp.sum((same & earlier).astype(jnp.int32), axis=1)
    return expert_ids * stride + offset + rank


def table_of(slots, slot_count):
    grid = jnp.arange(slot_count, dtype=jnp.int32)
    return (grid[:, None] == slots[None, :]).astype(jnp.bfloat16)


def run_kernel(body, out_shape, scratch, *operands, far=(), far_out=(), scalars=(), aliases={}):
    everywhere = pl.BlockSpec(memory_space=pltpu.HBM)
    near = pl.BlockSpec(memory_space=pltpu.VMEM)
    small = pl.BlockSpec(memory_space=pltpu.SMEM)
    in_specs = [
        small if k in scalars else everywhere if k in far else near for k in range(len(operands))
    ]
    leaves, treedef = jax.tree.flatten(out_shape)
    leaves = [
        pltpu.HBM(leaf.shape, leaf.dtype) if k in far_out else leaf
        for k, leaf in enumerate(leaves)
    ]
    out_specs = [everywhere if k in far_out else near for k in range(len(leaves))]
    return pl.pallas_call(
        body,
        out_shape=jax.tree.unflatten(treedef, leaves),
        in_specs=in_specs,
        out_specs=jax.tree.unflatten(treedef, out_specs),
        scratch_shapes=scratch,
        input_output_aliases=aliases,
        compiler_params=pltpu.CompilerParams(vmem_limit_bytes=40 * 1024 * 1024),
    )(*operands)


def array(shape, dtype=jnp.bfloat16):
    return jax.ShapeDtypeStruct(shape, dtype)


def unpack_slots(source, rows):
    count, depth, _ = source.shape
    for index in range(count):
        rows[depth * index : depth * (index + 1), :] = source[index].astype(jnp.float32)


def pack_slots(rows, target):
    count, depth, _ = target.shape
    for index in range(count):
        target[index] = rows[depth * index : depth * (index + 1), :].astype(jnp.bfloat16)


def normed_rows(values):
    widened = values.astype(jnp.float32)
    return (widened * rms_scale(values)).astype(jnp.bfloat16)


def send_body(values, table, target, rows):
    rows[...] = dot(table[...], normed_rows(values[...]))
    pack_slots(rows, target)


def take_rows(returned, pick_table, values, gate, result, rows):
    unpack_slots(returned, rows)
    gathered = dot(pick_table[...], rows[...].astype(jnp.bfloat16))
    result[...] = (values[...].astype(jnp.float32) + gate[...] * gathered).astype(jnp.bfloat16)


def keep(flag, copies, begin):
    @pl.when(flag[0] == 1)
    def _():
        for copy in copies:
            copy.start() if begin else copy.wait()


def take_body(flag, returned, pick_table, values, gate, old, result, record, rows, done):
    copies = [pltpu.make_async_copy(values, record, done.at[0])]
    keep(flag, copies, True)
    take_rows(returned, pick_table, values, gate, result, rows)
    keep(flag, copies, False)


def turn_body(
    flag, returned, pick_table, values, gate, old, table, result, record, target, rows, done
):
    copies = [pltpu.make_async_copy(values, record, done.at[0])]
    keep(flag, copies, True)
    take_rows(returned, pick_table, values, gate, result, rows)
    send_body(result, table, target, rows)
    keep(flag, copies, False)


def send_back_body(grads, gate, table, target, rows):
    grad_out = (gate[...] * grads[...].astype(jnp.float32)).astype(jnp.bfloat16)
    rows[...] = dot(table[...], grad_out)
    pack_slots(rows, target)


def take_back_body(returned, pick_table, record, grads, result, rows, values, done):
    load = pltpu.make_async_copy(record, values, done.at[0])
    load.start()
    unpack_slots(returned, rows)
    grad_norm = dot(pick_table[...], rows[...].astype(jnp.bfloat16))
    load.wait()
    value = values[...]
    result[...] = (
        grads[...].astype(jnp.float32) + norm_back(value, rms_scale(value), grad_norm)
    ).astype(jnp.bfloat16)


def turn_back_body(
    returned, pick_table, record, grads, gate, table, result, target, rows, values, done
):
    take_back_body(returned, pick_table, record, grads, result, rows, values, done)
    send_back_body(result, gate, table, target, rows)


def serve_body(
    flag,
    received,
    gate_mat,
    up_mat,
    down_mat,
    old_kept,
    old_pre,
    served,
    kept_record,
    pre_record,
    rows,
    kept,
    pre,
    done,
):
    unpack_slots(received, rows)
    kept[...] = rows[...].astype(jnp.bfloat16)
    first = [pltpu.make_async_copy(kept, kept_record, done.at[0])]
    keep(flag, first, True)
    pre[0] = dot(kept[...], gate_mat[...])
    pre[1] = dot(kept[...], up_mat[...])
    second = [pltpu.make_async_copy(pre, pre_record, done.at[1])]
    keep(flag, second, True)
    gate = pre[0]
    hidden = (gate * jax.nn.sigmoid(gate) * pre[1]).astype(jnp.bfloat16)
    rows[...] = dot(hidden, down_mat[...])
    pack_slots(rows, served)
    keep(flag, first + second, False)


def serve_back_rows(received, load, pre, down_mat, slot_grads, narrow, rows, begin):
    load.start()
    unpack_slots(received, rows)
    slot_grads[...] = rows[...].astype(jnp.bfloat16)
    begin()
    grad_hidden = dot_t(slot_grads[...], down_mat[...])
    load.wait()
    gate = pre[0]
    up = pre[1]
    gate_sig = jax.nn.sigmoid(gate)
    gate_act = gate * gate_sig
    grad_gate = (grad_hidden * up * (gate_sig * (1.0 + gate * (1.0 - gate_sig)))).astype(
        jnp.bfloat16
    )
    grad_up = (grad_hidden * gate_act).astype(jnp.bfloat16)
    inner = gate.shape[1]
    narrow[:, :inner] = (gate_act * up).astype(jnp.bfloat16)
    narrow[:, inner : 2 * inner] = grad_gate
    narrow[:, 2 * inner :] = grad_up
    return (grad_gate, grad_up)


def serve_back_body(
    flag,
    received,
    pre_record,
    gate_mat,
    up_mat,
    down_mat,
    old_grads,
    old_narrow,
    target,
    grads_record,
    narrow_record,
    rows,
    pre,
    slot_grads,
    narrow,
    done,
):
    load = pltpu.make_async_copy(pre_record, pre, done.at[0])
    first = [pltpu.make_async_copy(slot_grads, grads_record, done.at[1])]
    grad_gate, grad_up = serve_back_rows(
        received, load, pre, down_mat, slot_grads, narrow, rows, lambda: keep(flag, first, True)
    )
    second = [pltpu.make_async_copy(narrow, narrow_record, done.at[2])]
    keep(flag, second, True)
    rows[...] = dot_t(grad_gate, gate_mat[...]) + dot_t(grad_up, up_mat[...])
    pack_slots(rows, target)
    keep(flag, first + second, False)


def serve_last_body(received, pre_record, down_mat, slot_grads, narrow, rows, pre, done):
    load = pltpu.make_async_copy(pre_record, pre, done.at[0])
    serve_back_rows(received, load, pre, down_mat, slot_grads, narrow, rows, lambda: None)


def lowrank_body(
    rows, mats, targets, head, grads, all_normed, all_act, all_pre, all_grads, values, inner, scale
):
    count = mats.shape[0]
    values[0] = rows[...]

    def forward(step, carry):
        index = count - 1 - step
        value = values[step]
        row_scale = rms_scale(value)
        normed = (value.astype(jnp.float32) * row_scale).astype(jnp.bfloat16)
        inner_pre = dot(normed, mats[index, 0])
        act = (inner_pre * jax.nn.sigmoid(inner_pre)).astype(jnp.bfloat16)
        all_normed[index] = normed
        all_act[index] = act
        inner[index] = inner_pre
        scale[index] = row_scale
        values[step + 1] = (
            value.astype(jnp.float32) + dot_t(act, mats[index, 1])
        ).astype(jnp.bfloat16)
        return carry

    lax.fori_loop(0, count, forward, 0)
    final = values[count]
    row_scale = rms_scale(final)
    logits = row_scale * jnp.sum(final.astype(jnp.float32) * head[...], axis=1, keepdims=True)
    grad_logit = jax.nn.sigmoid(logits) - targets[...]
    grads[...] = norm_back(final, row_scale, grad_logit * head[...]).astype(jnp.bfloat16)

    def backward(index, carry):
        value = values[count - 1 - index]
        grad = grads[...]
        inner_pre = inner[index]
        inner_sig = jax.nn.sigmoid(inner_pre)
        grad_act = dot(grad, mats[index, 1])
        grad_pre = (grad_act * (inner_sig * (1.0 + inner_pre * (1.0 - inner_sig)))).astype(
            jnp.bfloat16
        )
        grad_norm = dot_t(grad_pre, mats[index, 0])
        all_pre[index] = grad_pre
        all_grads[index] = grad
        grads[...] = (
            grad.astype(jnp.float32) + norm_back(value, scale[index], grad_norm)
        ).astype(jnp.bfloat16)
        return carry

    lax.fori_loop(0, count, backward, 0)


def lowrank_layers(rows, mats, targets, head):
    count, rank = (mats.shape[0], mats.shape[3])
    row_count, width = rows.shape
    wide = array((count, row_count, width))
    narrow = array((count, row_count, rank))
    return run_kernel(
        lowrank_body,
        (array(rows.shape), wide, narrow, narrow, wide),
        [
            pltpu.VMEM((count + 1, row_count, width), jnp.bfloat16),
            pltpu.VMEM((count, row_count, rank), jnp.float32),
            pltpu.VMEM((count, row_count, 1), jnp.float32),
        ],
        rows,
        mats,
        targets,
        head,
    )


def exchange(buffer):
    return lax.all_to_all(buffer, "expert", split_axis=0, concat_axis=0, tiled=True)


def work_rows(slots, width):
    return [pltpu.VMEM((slots, width), jnp.float32)]


def packed_shape(table, width):
    count = lax.axis_size("expert")
    return array((count, table.shape[0] // count, width))


def send(values, table):
    width = values.shape[1]
    return run_kernel(
        send_body, packed_shape(table, width), work_rows(table.shape[0], width), values, table
    )


def take(flag, returned, route, values, record):
    table, pick_table, gate = route
    return run_kernel(
        take_body,
        (array(values.shape), array(record.shape)),
        work_rows(table.shape[0], values.shape[1]) + [pltpu.SemaphoreType.DMA((1,))],
        flag,
        returned,
        pick_table,
        values,
        gate,
        record,
        far=(5,),
        far_out=(1,),
        scalars=(0,),
        aliases={5: 1},
    )


def turn(flag, returned, route, values, record, next_table):
    table, pick_table, gate = route
    width = values.shape[1]
    return run_kernel(
        turn_body,
        (array(values.shape), array(record.shape), packed_shape(next_table, width)),
        work_rows(table.shape[0], width) + [pltpu.SemaphoreType.DMA((1,))],
        flag,
        returned,
        pick_table,
        values,
        gate,
        record,
        next_table,
        far=(5,),
        far_out=(1,),
        scalars=(0,),
        aliases={5: 1},
    )


def send_back(grads, route):
    table, _, gate = route
    width = grads.shape[1]
    return run_kernel(
        send_back_body,
        packed_shape(table, width),
        work_rows(table.shape[0], width),
        grads,
        gate,
        table,
    )


def load_rows(slots, values):
    return work_rows(slots, values.shape[1]) + [
        pltpu.VMEM(values.shape, jnp.bfloat16),
        pltpu.SemaphoreType.DMA((1,)),
    ]


def take_back(returned, route, values, grads):
    table, pick_table, _ = route
    return run_kernel(
        take_back_body,
        array(values.shape),
        load_rows(table.shape[0], values),
        returned,
        pick_table,
        values,
        grads,
        far=(2,),
    )


def turn_back(returned, route, values, grads, next_route):
    table, pick_table, _ = route
    return run_kernel(
        turn_back_body,
        (array(values.shape), packed_shape(next_route[0], values.shape[1])),
        load_rows(table.shape[0], values),
        returned,
        pick_table,
        values,
        grads,
        next_route[2],
        next_route[0],
        far=(2,),
    )


def serve(flag, received, mats, kept, pre):
    slots, width = kept.shape
    return run_kernel(
        serve_body,
        (array(received.shape), array(kept.shape), array(pre.shape, jnp.float32)),
        work_rows(slots, width)
        + [
            pltpu.VMEM(kept.shape, jnp.bfloat16),
            pltpu.VMEM(pre.shape, jnp.float32),
            pltpu.SemaphoreType.DMA((2,)),
        ],
        flag,
        received,
        *mats,
        kept,
        pre,
        far=(5, 6),
        far_out=(1, 2),
        scalars=(0,),
        aliases={5: 1, 6: 2},
    )


def serve_back(flag, received, pre, mats, grads, narrow):
    slots, width = grads.shape
    return run_kernel(
        serve_back_body,
        (array(received.shape), array(grads.shape), array(narrow.shape)),
        work_rows(slots, width)
        + [
            pltpu.VMEM(pre.shape, jnp.float32),
            pltpu.VMEM(grads.shape, jnp.bfloat16),
            pltpu.VMEM(narrow.shape, jnp.bfloat16),
            pltpu.SemaphoreType.DMA((3,)),
        ],
        flag,
        received,
        pre,
        *mats,
        grads,
        narrow,
        far=(2, 6, 7),
        far_out=(1, 2),
        scalars=(0,),
        aliases={6: 1, 7: 2},
    )


def serve_last(received, pre, down_mat):
    width = received.shape[2]
    _, slots, inner = pre.shape
    return run_kernel(
        serve_last_body,
        (array((slots, width)), array((slots, 3 * inner))),
        work_rows(slots, width)
        + [pltpu.VMEM(pre.shape, jnp.float32), pltpu.SemaphoreType.DMA((1,))],
        received,
        pre,
        down_mat,
        far=(1,),
    )


def local(
    features,
    labels,
    routes,
    route_gates,
    gate_weight,
    up_weight,
    down_weight,
    lowrank_in,
    lowrank_out,
    head_weight,
):
    section_count = lax.axis_size("section")
    section = lax.axis_index("section")
    expert_count = lax.axis_size("expert")
    micro_count, row_count, width = features.shape
    inner = gate_weight.shape[3]
    is_even = section % 2 == 0
    pair = section // 2
    to_odd = [(s, s + 1) for s in range(0, section_count, 2)]
    to_even = [(s + 1, s) for s in range(0, section_count, 2)]

    def swap(value):
        return lax.ppermute(value, "section", to_odd + to_even)

    def hop(value, layer):
        first = 0 if layer % 4 < 2 else 2
        links = []
        for start in range(first, first + section_count, 4):
            for lower in (start, start + 1):
                low_end, high_end = (lower % section_count, (lower + 2) % section_count)
                links += [(low_end, high_end), (high_end, low_end)]
        half = value.shape[0] // 2
        parts = [lax.ppermute(part, "section", links) for part in (value[:half], value[half:])]
        return jnp.concatenate(parts, axis=0)

    own = (gate_weight[0, 0], up_weight[0, 0], down_weight[0, 0])
    gate_other = swap(own[0])
    up_back = lax.ppermute(own[1], "section", to_even)
    down_back = lax.ppermute(own[2], "section", to_even)

    ids = routes[0, :, :, 0]
    plan = jnp.concatenate([ids.astype(jnp.float32), route_gates[0]], axis=0)
    plan_other = swap(plan)

    def route_of(slots, slot_count, gates):
        table = table_of(slots, slot_count)
        grid = jnp.arange(slot_count, dtype=jnp.int32)
        pick_table = (slots[:, None] == grid[None, :]).astype(jnp.bfloat16)
        return (table, pick_table, gates[:, None])

    def pick(first, second):
        chosen = jnp.where(is_even, first, second)
        mine = jnp.where(is_even, chosen[0::2], chosen[1::2])
        slots = slot_of_rows(mine[0].astype(jnp.int32), expert_count, capacity, 0)
        return route_of(slots, expert_count * capacity, mine[1])

    route_even = pick(plan, plan_other)
    route_odd = pick(plan_other, plan)
    joint_slots = jnp.concatenate(
        [
            slot_of_rows(ids[m], expert_count, capacity * micro_count, capacity * m)
            for m in range(micro_count)
        ]
    )
    route_all = route_of(
        joint_slots, expert_count * capacity * micro_count, route_gates[0].reshape(-1)
    )
    routing = [route_odd if layer % 2 else route_even for layer in range(section_count)]

    slot_count = expert_count * capacity

    def blank(*shape, dtype=jnp.bfloat16):
        return jnp.zeros(shape, dtype)

    flags = [(pair == layer // 2).astype(jnp.int32)[None] for layer in range(section_count)]
    always = jnp.ones((1,), jnp.int32)
    first_rows = features.reshape(-1, width)
    served, kept_all, pre_all = serve(
        always,
        exchange(send(first_rows, route_all[0])),
        own,
        blank(micro_count * slot_count, width),
        blank(2, micro_count * slot_count, inner, dtype=jnp.float32),
    )
    second_rows, _ = take(
        always, exchange(served), route_all, first_rows, blank(*first_rows.shape)
    )
    crossing = lax.ppermute(second_rows[row_count:], "section", to_odd)
    rows = jnp.where(is_even, second_rows[:row_count], crossing)
    sending = send(rows, routing[1][0])
    sending, gate_other, up_back, down_back, *late = lax.optimization_barrier(
        (sending, gate_other, up_back, down_back, *own)
    )
    back = (gate_other, up_back, down_back)
    mats_odd = tuple(jnp.where(is_even, b, a) for a, b in zip(own, back))
    up_on = lax.ppermute(late[1], "section", to_odd)
    down_on = lax.ppermute(late[2], "section", to_odd)

    row_record = [blank(row_count, width) for _ in range(2)]
    kept_record = [blank(slot_count, width) for _ in range(2)]
    pre_record = [blank(2, slot_count, inner, dtype=jnp.float32) for _ in range(2)]
    for layer in range(1, section_count):
        side = layer % 2
        if layer == 2:
            up_on, down_on, sending = lax.optimization_barrier((up_on, down_on, sending))
            on = (gate_other, up_on, down_on)
            mats_even = tuple(jnp.where(is_even, a, b) for a, b in zip(own, on))
        served, kept_record[side], pre_record[side] = serve(
            flags[layer],
            exchange(sending),
            mats_odd if side else mats_even,
            kept_record[side],
            pre_record[side],
        )
        returned = exchange(served)
        if side == 0:
            rows, row_record[side], sending = turn(
                flags[layer],
                returned,
                routing[layer],
                rows,
                row_record[side],
                routing[layer + 1][0],
            )
            if layer == 2:
                low_own = jnp.stack([lowrank_in[0], lowrank_out[0].T])
                low_own, rows = lax.optimization_barrier((low_own, rows))
                low_mats = lax.all_gather(low_own, "section")
        else:
            rows, row_record[side] = take(
                flags[layer], returned, routing[layer], rows, row_record[side]
            )
            if layer < section_count - 1:
                rows = hop(rows, layer)
                sending = send(rows, routing[layer + 1][0])
    mats = [mats_odd if layer % 2 else mats_even for layer in range(section_count)]

    targets = jnp.where(is_even, labels[0], labels[1]).astype(jnp.float32)[:, None]
    grads, low_normed, low_act, low_pre, low_grads = lowrank_layers(
        rows, low_mats, targets, head_weight[None, :]
    )
    sending = send_back(grads, routing[section_count - 1])
    sending, low_normed, low_act, low_pre, low_grads = lax.optimization_barrier(
        (sending, low_normed, low_act, low_pre, low_grads)
    )

    def low_part(wide, narrow):
        part = dot_tn(wide, narrow).astype(jnp.bfloat16)
        return part.reshape(expert_count, 1, -1, part.shape[1])

    parts = jnp.stack(
        [
            jnp.concatenate(
                [
                    low_part(low_normed[index], low_pre[index]),
                    low_part(low_grads[index], low_act[index]),
                ],
                axis=1,
            )
            for index in range(section_count)
        ],
        axis=1,
    )
    last_pair = section_count // 2 - 1
    parts = jnp.where(pair == last_pair, parts, jnp.zeros_like(parts))

    grads_record = [blank(slot_count, width) for _ in range(2)]
    narrow_record = [blank(slot_count, 3 * inner) for _ in range(2)]
    for layer in reversed(range(1, section_count)):
        side = layer % 2
        target, grads_record[side], narrow_record[side] = serve_back(
            flags[layer],
            exchange(sending),
            pre_record[side],
            mats[layer],
            grads_record[side],
            narrow_record[side],
        )
        returned = exchange(target)
        values = row_record[side]
        if side == 1 and layer > 1:
            grads, sending = turn_back(returned, routing[layer], values, grads, routing[layer - 1])
        else:
            grads = take_back(returned, routing[layer], values, grads)
        if layer == 6:
            parts, grads = lax.optimization_barrier((parts, grads))
            share = lax.psum_scatter(
                parts.reshape(-1, parts.shape[-1]), "expert", scatter_dimension=0, tiled=True
            ).reshape(parts.shape[1:])
        if layer == 2:
            share, grads = lax.optimization_barrier((share, grads))
            share = lax.all_to_all(share, "section", split_axis=0, concat_axis=0, tiled=True)
        if layer % 2 == 0:
            grads = hop(grads, layer - 2)
            sending = send_back(grads, routing[layer - 1])

    all_grads = jnp.concatenate([grads, lax.ppermute(grads, "section", to_even)], axis=0)
    saved = tuple(zip(kept_record, grads_record, narrow_record))
    theirs = tuple(swap(jnp.where(is_even, b, a)) for a, b in zip(*saved))
    held = tuple(jnp.where(is_even, a, b) for a, b in zip(*saved))
    joint = (kept_all,) + tuple(
        serve_last(exchange(send_back(all_grads, route_all)), pre_all, own[2])
    )
    kept, slot_grads, narrow = (
        jnp.where(section == 0, both, jnp.concatenate([mine, other], axis=0))
        for both, mine, other in zip(joint, held, theirs)
    )
    hidden, grad_gate, grad_up = (narrow[:, inner * k : inner * (k + 1)] for k in range(3))
    share = jnp.sum(share[2 * last_pair :].astype(jnp.float32), axis=0)
    return (
        dot_tn(kept, grad_gate)[None, None],
        dot_tn(kept, grad_up)[None, None],
        dot_tn(hidden, slot_grads)[None, None],
        share[0][None],
        share[1].T[None],
    )


def solution(mesh):
    return jax.shard_map(
        local,
        mesh=mesh,
        in_specs=(
            P(None, "expert", None),
            P(None, "expert"),
            P("section", None, "expert", None),
            P("section", None, "expert"),
            P("section", "expert", None, None),
            P("section", "expert", None, None),
            P("section", "expert", None, None),
            P("section", None, None),
            P("section", None, None),
            P(),
        ),
        out_specs=(
            P("section", "expert", None, None),
            P("section", "expert", None, None),
            P("section", "expert", None, None),
            P("section", "expert", None),
            P("section", None, "expert"),
        ),
        check_vma=False,
    )
```

```python
import jax
import jax.numpy as jnp
from jax import lax
from jax.experimental import pallas as pl
from jax.experimental.pallas import tpu as pltpu
from jax.sharding import PartitionSpec as P

epsilon = 1e-06
capacity = 3


def dot(left, right):
    return jnp.dot(left, right, preferred_element_type=jnp.float32)


def dot_t(left, right):
    return lax.dot_general(left, right, (((1,), (1,)), ((), ())), preferred_element_type=jnp.float32)


def dot_tn(left, right):
    return lax.dot_general(left, right, (((0,), (0,)), ((), ())), preferred_element_type=jnp.float32)


def rms_scale(values):
    widened = values.astype(jnp.float32)
    return lax.rsqrt(jnp.mean(widened * widened, axis=-1, keepdims=True) + epsilon)


def norm_back(values, row_scale, grad_norm):
    widened = values.astype(jnp.float32)
    inner_mean = jnp.mean(grad_norm * widened, axis=-1, keepdims=True)
    return row_scale * grad_norm - widened * (row_scale * row_scale * row_scale) * inner_mean


def slot_of_rows(expert_ids, expert_count, stride, offset):
    chosen = (expert_ids[:, None] == jnp.arange(expert_count, dtype=jnp.int32)[None, :]).astype(
        jnp.int32
    )
    earlier = jnp.arange(expert_ids.shape[0])[:, None] > jnp.arange(expert_ids.shape[0])[None, :]
    same = expert_ids[:, None] == expert_ids[None, :]
    rank = jnp.sum((same & earlier).astype(jnp.int32), axis=1)
    return expert_ids * stride + offset + rank


def table_of(slots, slot_count):
    grid = jnp.arange(slot_count, dtype=jnp.int32)
    return (grid[:, None] == slots[None, :]).astype(jnp.bfloat16)


def run_kernel(
    body, out_shape, scratch, *operands, far=(), far_out=(), scalars=(), aliases={}, limit=16
):
    absent = [k for k, operand in enumerate(operands) if operand is None]
    if absent:
        count, inner_body = (len(operands), body)
        operands = [operand for operand in operands if operand is not None]
        shift = {
            k: k - sum(gone < k for gone in absent) for k in range(count) if k not in absent
        }
        far, scalars = (tuple(shift[k] for k in group if k in shift) for group in (far, scalars))
        aliases = {shift[k]: out for k, out in aliases.items() if k in shift}

        def body(*refs):
            refs = iter(refs)
            given = [None if k in absent else next(refs) for k in range(count)]
            inner_body(*given, *refs)

    everywhere = pl.BlockSpec(memory_space=pltpu.HBM)
    near = pl.BlockSpec(memory_space=pltpu.VMEM)
    small = pl.BlockSpec(memory_space=pltpu.SMEM)
    in_specs = [
        small if k in scalars else everywhere if k in far else near for k in range(len(operands))
    ]
    leaves, treedef = jax.tree.flatten(out_shape)
    leaves = [
        pltpu.HBM(leaf.shape, leaf.dtype) if k in far_out else leaf
        for k, leaf in enumerate(leaves)
    ]
    out_specs = [everywhere if k in far_out else near for k in range(len(leaves))]
    return pl.pallas_call(
        body,
        out_shape=jax.tree.unflatten(treedef, leaves),
        in_specs=in_specs,
        out_specs=jax.tree.unflatten(treedef, out_specs),
        scratch_shapes=scratch,
        input_output_aliases=aliases,
        compiler_params=pltpu.CompilerParams(vmem_limit_bytes=limit * 1024 * 1024),
    )(*operands)


def array(shape, dtype=jnp.bfloat16):
    return jax.ShapeDtypeStruct(shape, dtype)


def unpack_slots(source, rows):
    count, depth, _ = source.shape
    for index in range(count):
        rows[depth * index : depth * (index + 1), :] = source[index].astype(jnp.float32)


def pack_slots(rows, target):
    count, depth, _ = target.shape
    for index in range(count):
        target[index] = rows[depth * index : depth * (index + 1), :].astype(jnp.bfloat16)


def normed_rows(values):
    widened = values.astype(jnp.float32)
    return (widened * rms_scale(values)).astype(jnp.bfloat16)


def send_body(values, table, target, rows):
    rows[...] = dot(table[...], normed_rows(values[...]))
    pack_slots(rows, target)


def take_rows(returned, pick_table, values, gate, result, rows):
    unpack_slots(returned, rows)
    gathered = dot(pick_table[...], rows[...].astype(jnp.bfloat16))
    result[...] = (values[...].astype(jnp.float32) + gate[...] * gathered).astype(jnp.bfloat16)


def keep(flag, copies, begin):
    @pl.when(flag[0] == 1)
    def _():
        for copy in copies:
            copy.start() if begin else copy.wait()


def take_body(flag, returned, pick_table, values, gate, old, result, record, rows, done):
    copies = [pltpu.make_async_copy(values, record, done.at[0])]
    keep(flag, copies, True)
    take_rows(returned, pick_table, values, gate, result, rows)
    keep(flag, copies, False)


def turn_body(
    flag, returned, pick_table, values, gate, old, table, result, record, target, rows, done
):
    copies = [pltpu.make_async_copy(values, record, done.at[0])]
    keep(flag, copies, True)
    take_rows(returned, pick_table, values, gate, result, rows)
    send_body(result, table, target, rows)
    keep(flag, copies, False)


def send_back_body(grads, gate, table, target, rows):
    grad_out = (gate[...] * grads[...].astype(jnp.float32)).astype(jnp.bfloat16)
    rows[...] = dot(table[...], grad_out)
    pack_slots(rows, target)


def take_back_body(returned, pick_table, record, grads, result, rows, values, done):
    load = pltpu.make_async_copy(record, values, done.at[0])
    load.start()
    unpack_slots(returned, rows)
    grad_norm = dot(pick_table[...], rows[...].astype(jnp.bfloat16))
    load.wait()
    value = values[...]
    result[...] = (
        grads[...].astype(jnp.float32) + norm_back(value, rms_scale(value), grad_norm)
    ).astype(jnp.bfloat16)


def turn_back_body(
    returned, pick_table, record, grads, gate, table, result, target, rows, values, done
):
    take_back_body(returned, pick_table, record, grads, result, rows, values, done)
    send_back_body(result, gate, table, target, rows)


def serve_body(
    flag,
    received,
    gate_mat,
    up_mat,
    down_mat,
    old_kept,
    old_pre,
    served,
    kept_record,
    pre_record,
    rows,
    kept,
    pre,
    done,
):
    unpack_slots(received, rows)
    kept[...] = rows[...].astype(jnp.bfloat16)
    first = [pltpu.make_async_copy(kept, kept_record, done.at[0])]
    keep(flag, first, True)
    pre[0] = dot(kept[...], gate_mat[...])
    pre[1] = dot(kept[...], up_mat[...])
    second = [pltpu.make_async_copy(pre, pre_record, done.at[1])]
    keep(flag, second, True)
    gate = pre[0]
    hidden = (gate * jax.nn.sigmoid(gate) * pre[1]).astype(jnp.bfloat16)
    rows[...] = dot(hidden, down_mat[...])
    pack_slots(rows, served)
    keep(flag, first + second, False)


def serve_back_rows(received, load, pre, down_mat, slot_grads, narrow, rows, begin):
    load.start()
    unpack_slots(received, rows)
    slot_grads[...] = rows[...].astype(jnp.bfloat16)
    begin()
    grad_hidden = dot_t(slot_grads[...], down_mat[...])
    load.wait()
    gate = pre[0]
    up = pre[1]
    gate_sig = jax.nn.sigmoid(gate)
    gate_act = gate * gate_sig
    grad_gate = (grad_hidden * up * (gate_sig * (1.0 + gate * (1.0 - gate_sig)))).astype(
        jnp.bfloat16
    )
    grad_up = (grad_hidden * gate_act).astype(jnp.bfloat16)
    inner = gate.shape[1]
    narrow[:, :inner] = (gate_act * up).astype(jnp.bfloat16)
    narrow[:, inner : 2 * inner] = grad_gate
    narrow[:, 2 * inner :] = grad_up
    return (grad_gate, grad_up)


def serve_back_body(
    flag,
    received,
    pre_record,
    gate_mat,
    up_mat,
    down_mat,
    old_grads,
    old_narrow,
    target,
    grads_record,
    narrow_record,
    rows,
    pre,
    slot_grads,
    narrow,
    done,
):
    load = pltpu.make_async_copy(pre_record, pre, done.at[0])
    first = [pltpu.make_async_copy(slot_grads, grads_record, done.at[1])]
    grad_gate, grad_up = serve_back_rows(
        received, load, pre, down_mat, slot_grads, narrow, rows, lambda: keep(flag, first, True)
    )
    second = [pltpu.make_async_copy(narrow, narrow_record, done.at[2])]
    keep(flag, second, True)
    rows[...] = dot_t(grad_gate, gate_mat[...]) + dot_t(grad_up, up_mat[...])
    pack_slots(rows, target)
    keep(flag, first + second, False)


def serve_last_body(received, pre_record, down_mat, slot_grads, narrow, rows, pre, done):
    load = pltpu.make_async_copy(pre_record, pre, done.at[0])
    serve_back_rows(received, load, pre, down_mat, slot_grads, narrow, rows, lambda: None)


def lowrank_body(
    flag, rows, mats, targets, head, grads, all_normed, all_act, all_pre, all_grads, values, inner, scale
):
    count = mats.shape[0]
    live = flag[0].astype(jnp.float32)
    values[0] = rows[...]

    def forward(step, carry):
        index = count - 1 - step
        value = values[step]
        row_scale = rms_scale(value)
        normed = (value.astype(jnp.float32) * row_scale).astype(jnp.bfloat16)
        inner_pre = dot(normed, mats[index, 0])
        act = (inner_pre * jax.nn.sigmoid(inner_pre)).astype(jnp.bfloat16)
        all_normed[index] = normed
        all_act[index] = (act.astype(jnp.float32) * live).astype(jnp.bfloat16)
        inner[index] = inner_pre
        scale[index] = row_scale
        values[step + 1] = (
            value.astype(jnp.float32) + dot_t(act, mats[index, 1])
        ).astype(jnp.bfloat16)
        return carry

    lax.fori_loop(0, count, forward, 0)
    final = values[count]
    row_scale = rms_scale(final)
    logits = row_scale * jnp.sum(final.astype(jnp.float32) * head[...], axis=1, keepdims=True)
    grad_logit = jax.nn.sigmoid(logits) - targets[...]
    grads[...] = norm_back(final, row_scale, grad_logit * head[...]).astype(jnp.bfloat16)

    def backward(index, carry):
        value = values[count - 1 - index]
        grad = grads[...]
        inner_pre = inner[index]
        inner_sig = jax.nn.sigmoid(inner_pre)
        grad_act = dot(grad, mats[index, 1])
        grad_pre = (grad_act * (inner_sig * (1.0 + inner_pre * (1.0 - inner_sig)))).astype(
            jnp.bfloat16
        )
        grad_norm = dot_t(grad_pre, mats[index, 0])
        all_pre[index] = (grad_pre.astype(jnp.float32) * live).astype(jnp.bfloat16)
        all_grads[index] = grad
        grads[...] = (
            grad.astype(jnp.float32) + norm_back(value, scale[index], grad_norm)
        ).astype(jnp.bfloat16)
        return carry

    lax.fori_loop(0, count, backward, 0)


def lowrank_layers(flag, rows, mats, targets, head):
    count, rank = (mats.shape[0], mats.shape[3])
    row_count, width = rows.shape
    wide = array((count, row_count, width))
    narrow = array((count, row_count, rank))
    return run_kernel(
        lowrank_body,
        (array(rows.shape), wide, narrow, narrow, wide),
        [
            pltpu.VMEM((count + 1, row_count, width), jnp.bfloat16),
            pltpu.VMEM((count, row_count, rank), jnp.float32),
            pltpu.VMEM((count, row_count, 1), jnp.float32),
        ],
        flag,
        rows,
        mats,
        targets,
        head,
        scalars=(0,),
        limit=40,
    )


def parts_body(normed, pre, grads, act, parts):
    blocks, _, _, depth, rank = parts.shape
    for kind, (wide, narrow) in enumerate(((normed, pre), (grads, act))):
        part = dot_tn(wide[0], narrow[0]).astype(jnp.bfloat16)
        parts[:, 0, kind] = part.reshape(blocks, depth, rank)


def lowrank_sums(normed, pre, grads, act, blocks):
    count, row_count, width = normed.shape
    rank = pre.shape[2]
    wide = pl.BlockSpec((1, row_count, width), lambda k: (k, 0, 0))
    narrow = pl.BlockSpec((1, row_count, rank), lambda k: (k, 0, 0))
    depth = width // blocks
    return pl.pallas_call(
        parts_body,
        grid=(count,),
        out_shape=array((blocks, count, 2, depth, rank)),
        in_specs=[wide, narrow, wide, narrow],
        out_specs=pl.BlockSpec((blocks, 1, 2, depth, rank), lambda k: (0, k, 0, 0, 0)),
        compiler_params=pltpu.CompilerParams(vmem_limit_bytes=16 * 1024 * 1024),
        cost_estimate=pl.CostEstimate(
            flops=4 * count * row_count * width * rank,
            bytes_accessed=4 * count * width * (row_count + rank),
            transcendentals=0,
        ),
    )(normed, pre, grads, act)


def exchange(buffer):
    return lax.all_to_all(buffer, "expert", split_axis=0, concat_axis=0, tiled=True)


def work_rows(slots, width):
    return [pltpu.VMEM((slots, width), jnp.float32)]


def packed_shape(table, width):
    count = lax.axis_size("expert")
    return array((count, table.shape[0] // count, width))


def send(values, table):
    width = values.shape[1]
    return run_kernel(
        send_body, packed_shape(table, width), work_rows(table.shape[0], width), values, table
    )


def take(flag, returned, route, values, record):
    table, pick_table, gate = route
    return run_kernel(
        take_body,
        (array(values.shape), array(values.shape)),
        work_rows(table.shape[0], values.shape[1]) + [pltpu.SemaphoreType.DMA((1,))],
        flag,
        returned,
        pick_table,
        values,
        gate,
        record,
        far=(5,),
        far_out=(1,),
        scalars=(0,),
        aliases={5: 1},
    )


def turn(flag, returned, route, values, record, next_table):
    table, pick_table, gate = route
    width = values.shape[1]
    return run_kernel(
        turn_body,
        (array(values.shape), array(values.shape), packed_shape(next_table, width)),
        work_rows(table.shape[0], width) + [pltpu.SemaphoreType.DMA((1,))],
        flag,
        returned,
        pick_table,
        values,
        gate,
        record,
        next_table,
        far=(5,),
        far_out=(1,),
        scalars=(0,),
        aliases={5: 1},
    )


def send_back(grads, route):
    table, _, gate = route
    width = grads.shape[1]
    return run_kernel(
        send_back_body,
        packed_shape(table, width),
        work_rows(table.shape[0], width),
        grads,
        gate,
        table,
    )


def load_rows(slots, values):
    return work_rows(slots, values.shape[1]) + [
        pltpu.VMEM(values.shape, jnp.bfloat16),
        pltpu.SemaphoreType.DMA((1,)),
    ]


def take_back(returned, route, values, grads):
    table, pick_table, _ = route
    return run_kernel(
        take_back_body,
        array(values.shape),
        load_rows(table.shape[0], values),
        returned,
        pick_table,
        values,
        grads,
        far=(2,),
    )


def turn_back(returned, route, values, grads, next_route):
    table, pick_table, _ = route
    return run_kernel(
        turn_back_body,
        (array(values.shape), packed_shape(next_route[0], values.shape[1])),
        load_rows(table.shape[0], values),
        returned,
        pick_table,
        values,
        grads,
        next_route[2],
        next_route[0],
        far=(2,),
    )


def serve(flag, received, mats, kept, pre):
    count, depth, width = received.shape
    slots, inner = (count * depth, mats[0].shape[1])
    return run_kernel(
        serve_body,
        (array(received.shape), array((slots, width)), array((2, slots, inner), jnp.float32)),
        work_rows(slots, width)
        + [
            pltpu.VMEM((slots, width), jnp.bfloat16),
            pltpu.VMEM((2, slots, inner), jnp.float32),
            pltpu.SemaphoreType.DMA((2,)),
        ],
        flag,
        received,
        *mats,
        kept,
        pre,
        far=(5, 6),
        far_out=(1, 2),
        scalars=(0,),
        aliases={5: 1, 6: 2},
    )


def serve_back(flag, received, pre, mats, grads, narrow):
    width = received.shape[2]
    _, slots, inner = pre.shape
    return run_kernel(
        serve_back_body,
        (array(received.shape), array((slots, width)), array((slots, 3 * inner))),
        work_rows(slots, width)
        + [
            pltpu.VMEM(pre.shape, jnp.float32),
            pltpu.VMEM((slots, width), jnp.bfloat16),
            pltpu.VMEM((slots, 3 * inner), jnp.bfloat16),
            pltpu.SemaphoreType.DMA((3,)),
        ],
        flag,
        received,
        pre,
        *mats,
        grads,
        narrow,
        far=(2, 6, 7),
        far_out=(1, 2),
        scalars=(0,),
        aliases={6: 1, 7: 2},
    )


def serve_last(received, pre, down_mat):
    width = received.shape[2]
    _, slots, inner = pre.shape
    return run_kernel(
        serve_last_body,
        (array((slots, width)), array((slots, 3 * inner))),
        work_rows(slots, width)
        + [pltpu.VMEM(pre.shape, jnp.float32), pltpu.SemaphoreType.DMA((1,))],
        received,
        pre,
        down_mat,
        far=(1,),
    )


def local(
    features,
    labels,
    routes,
    route_gates,
    gate_weight,
    up_weight,
    down_weight,
    lowrank_in,
    lowrank_out,
    head_weight,
):
    section_count = lax.axis_size("section")
    section = lax.axis_index("section")
    expert_count = lax.axis_size("expert")
    micro_count, row_count, width = features.shape
    inner = gate_weight.shape[3]
    is_even = section % 2 == 0
    pair = section // 2
    to_odd = [(s, s + 1) for s in range(0, section_count, 2)]
    to_even = [(s + 1, s) for s in range(0, section_count, 2)]

    def swap(value):
        return lax.ppermute(value, "section", to_odd + to_even)

    def hop(value, layer):
        first = 0 if layer % 4 < 2 else 2
        links = []
        for start in range(first, first + section_count, 4):
            for lower in (start, start + 1):
                low_end, high_end = (lower % section_count, (lower + 2) % section_count)
                links += [(low_end, high_end), (high_end, low_end)]
        half = value.shape[0] // 2
        parts = [lax.ppermute(part, "section", links) for part in (value[:half], value[half:])]
        return jnp.concatenate(parts, axis=0)

    own = (gate_weight[0, 0], up_weight[0, 0], down_weight[0, 0])
    gate_other, up_other = (swap(own[0]), swap(own[1]))

    ids = routes[0, :, :, 0]
    plan = jnp.concatenate([ids.astype(jnp.float32), route_gates[0]], axis=0)
    plan_other = swap(plan)

    def route_of(slots, slot_count, gates):
        table = table_of(slots, slot_count)
        grid = jnp.arange(slot_count, dtype=jnp.int32)
        pick_table = (slots[:, None] == grid[None, :]).astype(jnp.bfloat16)
        return (table, pick_table, gates[:, None])

    def pick(first, second):
        chosen = jnp.where(is_even, first, second)
        mine = jnp.where(is_even, chosen[0::2], chosen[1::2])
        slots = slot_of_rows(mine[0].astype(jnp.int32), expert_count, capacity, 0)
        return route_of(slots, expert_count * capacity, mine[1])

    route_even = pick(plan, plan_other)
    route_odd = pick(plan_other, plan)
    joint_slots = jnp.concatenate(
        [
            slot_of_rows(ids[m], expert_count, capacity * micro_count, capacity * m)
            for m in range(micro_count)
        ]
    )
    route_all = route_of(
        joint_slots, expert_count * capacity * micro_count, route_gates[0].reshape(-1)
    )
    routing = [route_odd if layer % 2 else route_even for layer in range(section_count)]

    flags = [(pair == layer // 2).astype(jnp.int32)[None] for layer in range(section_count)]
    always = jnp.ones((1,), jnp.int32)
    first_rows = features.reshape(-1, width)
    served, kept_all, pre_all = serve(
        always, exchange(send(first_rows, route_all[0])), own, None, None
    )
    second_rows, _ = take(always, exchange(served), route_all, first_rows, None)
    second_rows, late = lax.optimization_barrier((second_rows, own[2]))
    crossing = lax.ppermute(second_rows[row_count:], "section", to_odd)
    down_back = lax.ppermute(late, "section", to_even)
    rows = jnp.where(is_even, second_rows[:row_count], crossing)
    rows, late = lax.optimization_barrier((rows, own[2]))
    down_on = lax.ppermute(late, "section", to_odd)
    sending = send(rows, routing[1][0])
    sending, gate_other, up_other = lax.optimization_barrier((sending, gate_other, up_other))
    others = (gate_other, up_other)
    mats_odd = tuple(jnp.where(is_even, b, a) for a, b in zip(own, others + (down_back,)))

    row_record = [None, None]
    kept_record = [None, None]
    pre_record = [None, None]
    for layer in range(1, section_count):
        side = layer % 2
        served, kept_record[side], pre_record[side] = serve(
            flags[layer],
            exchange(sending),
            mats_odd if side else mats_even,
            kept_record[side],
            pre_record[side],
        )
        if layer == 1:
            served, down_on = lax.optimization_barrier((served, down_on))
            mats_even = tuple(jnp.where(is_even, a, b) for a, b in zip(own, others + (down_on,)))
        returned = exchange(served)
        if side == 0:
            rows, row_record[side], sending = turn(
                flags[layer],
                returned,
                routing[layer],
                rows,
                row_record[side],
                routing[layer + 1][0],
            )
            if layer == 2:
                low_own = jnp.stack([lowrank_in[0], lowrank_out[0].T])
                low_own, rows = lax.optimization_barrier((low_own, rows))
                low_mats = lax.all_gather(low_own, "section")
        else:
            rows, row_record[side] = take(
                flags[layer], returned, routing[layer], rows, row_record[side]
            )
            if layer < section_count - 1:
                rows = hop(rows, layer)
                sending = send(rows, routing[layer + 1][0])
    mats = [mats_odd if layer % 2 else mats_even for layer in range(section_count)]

    targets = jnp.where(is_even, labels[0], labels[1]).astype(jnp.float32)[:, None]
    grads, low_normed, low_act, low_pre, low_grads = lowrank_layers(
        flags[-1], rows, low_mats, targets, head_weight[None, :]
    )
    sending = send_back(grads, routing[section_count - 1])
    sending, low_normed, low_act, low_pre, low_grads = lax.optimization_barrier(
        (sending, low_normed, low_act, low_pre, low_grads)
    )

    parts = lowrank_sums(low_normed, low_pre, low_grads, low_act, expert_count)
    last_pair = section_count // 2 - 1

    grads_record = [None, None]
    narrow_record = [None, None]
    for layer in reversed(range(1, section_count)):
        side = layer % 2
        target, grads_record[side], narrow_record[side] = serve_back(
            flags[layer],
            exchange(sending),
            pre_record[side],
            mats[layer],
            grads_record[side],
            narrow_record[side],
        )
        returned = exchange(target)
        values = row_record[side]
        if side == 1 and layer > 1:
            grads, sending = turn_back(returned, routing[layer], values, grads, routing[layer - 1])
        else:
            grads = take_back(returned, routing[layer], values, grads)
        if layer == section_count - 1:
            parts, sending = lax.optimization_barrier((parts, sending))
            share = lax.psum_scatter(
                parts.reshape(-1, parts.shape[-1]), "expert", scatter_dimension=0, tiled=True
            ).reshape(parts.shape[1:])
        if layer == 2:
            share, grads = lax.optimization_barrier((share, grads))
            share = lax.all_to_all(share, "section", split_axis=0, concat_axis=0, tiled=True)
        if layer % 2 == 0:
            grads = hop(grads, layer - 2)
            sending = send_back(grads, routing[layer - 1])

    all_grads = jnp.concatenate([grads, lax.ppermute(grads, "section", to_even)], axis=0)
    saved = tuple(zip(kept_record, grads_record, narrow_record))
    theirs = tuple(swap(jnp.where(is_even, b, a)) for a, b in zip(*saved))
    held = tuple(jnp.where(is_even, a, b) for a, b in zip(*saved))
    joint = (kept_all,) + tuple(
        serve_last(exchange(send_back(all_grads, route_all)), pre_all, own[2])
    )
    kept, slot_grads, narrow = (
        jnp.where(section == 0, both, jnp.concatenate([mine, other], axis=0))
        for both, mine, other in zip(joint, held, theirs)
    )
    hidden, grad_gate, grad_up = (narrow[:, inner * k : inner * (k + 1)] for k in range(3))
    share = jnp.sum(share[2 * last_pair :].astype(jnp.float32), axis=0)
    return (
        dot_tn(kept, grad_gate)[None, None],
        dot_tn(kept, grad_up)[None, None],
        dot_tn(hidden, slot_grads)[None, None],
        share[0][None],
        share[1].T[None],
    )


def solution(mesh):
    return jax.shard_map(
        local,
        mesh=mesh,
        in_specs=(
            P(None, "expert", None),
            P(None, "expert"),
            P("section", None, "expert", None),
            P("section", None, "expert"),
            P("section", "expert", None, None),
            P("section", "expert", None, None),
            P("section", "expert", None, None),
            P("section", None, None),
            P("section", None, None),
            P(),
        ),
        out_specs=(
            P("section", "expert", None, None),
            P("section", "expert", None, None),
            P("section", "expert", None, None),
            P("section", "expert", None),
            P("section", None, "expert"),
        ),
        check_vma=False,
    )
```

```python
import jax
import jax.numpy as jnp
from jax import lax
from jax.experimental import pallas as pl
from jax.experimental.pallas import tpu as pltpu
from jax.sharding import PartitionSpec as P

epsilon = 1e-06
capacity = 3


def dot(left, right):
    return jnp.dot(left, right, preferred_element_type=jnp.float32)


def dot_t(left, right):
    return lax.dot_general(left, right, (((1,), (1,)), ((), ())), preferred_element_type=jnp.float32)


def dot_tn(left, right):
    return lax.dot_general(left, right, (((0,), (0,)), ((), ())), preferred_element_type=jnp.float32)


def rms_scale(values):
    widened = values.astype(jnp.float32)
    return lax.rsqrt(jnp.mean(widened * widened, axis=-1, keepdims=True) + epsilon)


def norm_back(values, row_scale, grad_norm):
    widened = values.astype(jnp.float32)
    inner_mean = jnp.mean(grad_norm * widened, axis=-1, keepdims=True)
    return row_scale * grad_norm - widened * (row_scale * row_scale * row_scale) * inner_mean


def slot_of_rows(expert_ids, expert_count, stride, offset):
    chosen = (expert_ids[:, None] == jnp.arange(expert_count, dtype=jnp.int32)[None, :]).astype(
        jnp.int32
    )
    earlier = jnp.arange(expert_ids.shape[0])[:, None] > jnp.arange(expert_ids.shape[0])[None, :]
    same = expert_ids[:, None] == expert_ids[None, :]
    rank = jnp.sum((same & earlier).astype(jnp.int32), axis=1)
    return expert_ids * stride + offset + rank


def table_of(slots, slot_count):
    grid = jnp.arange(slot_count, dtype=jnp.int32)
    return (grid[:, None] == slots[None, :]).astype(jnp.bfloat16)


def run_kernel(
    body, out_shape, scratch, *operands, far=(), far_out=(), scalars=(), aliases={}, limit=16
):
    absent = [k for k, operand in enumerate(operands) if operand is None]
    if absent:
        count, inner_body = (len(operands), body)
        operands = [operand for operand in operands if operand is not None]
        shift = {
            k: k - sum(gone < k for gone in absent) for k in range(count) if k not in absent
        }
        far, scalars = (tuple(shift[k] for k in group if k in shift) for group in (far, scalars))
        aliases = {shift[k]: out for k, out in aliases.items() if k in shift}

        def body(*refs):
            refs = iter(refs)
            given = [None if k in absent else next(refs) for k in range(count)]
            inner_body(*given, *refs)

    everywhere = pl.BlockSpec(memory_space=pltpu.HBM)
    near = pl.BlockSpec(memory_space=pltpu.VMEM)
    small = pl.BlockSpec(memory_space=pltpu.SMEM)
    in_specs = [
        small if k in scalars else everywhere if k in far else near for k in range(len(operands))
    ]
    leaves, treedef = jax.tree.flatten(out_shape)
    leaves = [
        pltpu.HBM(leaf.shape, leaf.dtype) if k in far_out else leaf
        for k, leaf in enumerate(leaves)
    ]
    out_specs = [everywhere if k in far_out else near for k in range(len(leaves))]
    return pl.pallas_call(
        body,
        out_shape=jax.tree.unflatten(treedef, leaves),
        in_specs=in_specs,
        out_specs=jax.tree.unflatten(treedef, out_specs),
        scratch_shapes=scratch,
        input_output_aliases=aliases,
        compiler_params=pltpu.CompilerParams(vmem_limit_bytes=limit * 1024 * 1024),
    )(*operands)


def array(shape, dtype=jnp.bfloat16):
    return jax.ShapeDtypeStruct(shape, dtype)


def unpack_slots(source, rows):
    count, depth, _ = source.shape
    for index in range(count):
        rows[depth * index : depth * (index + 1), :] = source[index].astype(jnp.float32)


def pack_slots(rows, target):
    count, depth, _ = target.shape
    for index in range(count):
        target[index] = rows[depth * index : depth * (index + 1), :].astype(jnp.bfloat16)


def normed_rows(values):
    widened = values.astype(jnp.float32)
    return (widened * rms_scale(values)).astype(jnp.bfloat16)


def send_body(values, table, target, rows):
    rows[...] = dot(table[...], normed_rows(values[...]))
    pack_slots(rows, target)


def take_rows(returned, pick_table, values, gate, result, rows):
    unpack_slots(returned, rows)
    gathered = dot(pick_table[...], rows[...].astype(jnp.bfloat16))
    result[...] = (values[...].astype(jnp.float32) + gate[...] * gathered).astype(jnp.bfloat16)


def keep(flag, copies, begin):
    @pl.when(flag[0] == 1)
    def _():
        for copy in copies:
            copy.start() if begin else copy.wait()


def take_body(flag, returned, pick_table, values, gate, old, result, record, rows, done):
    copies = [pltpu.make_async_copy(values, record, done.at[0])]
    keep(flag, copies, True)
    take_rows(returned, pick_table, values, gate, result, rows)
    keep(flag, copies, False)


def turn_body(
    flag, returned, pick_table, values, gate, old, table, result, record, target, rows, done
):
    copies = [pltpu.make_async_copy(values, record, done.at[0])]
    keep(flag, copies, True)
    take_rows(returned, pick_table, values, gate, result, rows)
    send_body(result, table, target, rows)
    keep(flag, copies, False)


def send_back_body(grads, gate, table, target, rows):
    grad_out = (gate[...] * grads[...].astype(jnp.float32)).astype(jnp.bfloat16)
    rows[...] = dot(table[...], grad_out)
    pack_slots(rows, target)


def take_back_body(returned, pick_table, record, grads, result, rows, values, done):
    load = pltpu.make_async_copy(record, values, done.at[0])
    load.start()
    unpack_slots(returned, rows)
    grad_norm = dot(pick_table[...], rows[...].astype(jnp.bfloat16))
    load.wait()
    value = values[...]
    result[...] = (
        grads[...].astype(jnp.float32) + norm_back(value, rms_scale(value), grad_norm)
    ).astype(jnp.bfloat16)


def turn_back_body(
    returned, pick_table, record, grads, gate, table, result, target, rows, values, done
):
    take_back_body(returned, pick_table, record, grads, result, rows, values, done)
    send_back_body(result, gate, table, target, rows)


def serve_body(
    flag,
    received,
    gate_mat,
    up_mat,
    down_mat,
    old_kept,
    old_pre,
    served,
    kept_record,
    pre_record,
    rows,
    kept,
    pre,
    done,
    ready=lambda index: None,
):
    unpack_slots(received, rows)
    kept[...] = rows[...].astype(jnp.bfloat16)
    first = [pltpu.make_async_copy(kept, kept_record, done.at[0])]
    keep(flag, first, True)
    ready(0)
    pre[0] = dot(kept[...], gate_mat[...])
    ready(1)
    pre[1] = dot(kept[...], up_mat[...])
    second = [pltpu.make_async_copy(pre, pre_record, done.at[1])]
    keep(flag, second, True)
    gate = pre[0]
    hidden = (gate * jax.nn.sigmoid(gate) * pre[1]).astype(jnp.bfloat16)
    ready(2)
    rows[...] = dot(hidden, down_mat[...])
    pack_slots(rows, served)
    keep(flag, first + second, False)


def fetch(sources, targets, done):
    copies = [
        pltpu.make_async_copy(source, target, done.at[index])
        for index, (source, target) in enumerate(zip(sources, targets))
    ]
    for copy in copies:
        copy.start()
    return lambda index: copies[index].wait()


def serve_far_body(flag, received, *refs):
    sources, refs, mats, loaded = (refs[:3], refs[3:-4], refs[-4:-1], refs[-1])
    old, outs, work = (refs[:2], refs[2:5], refs[8:])
    ready = fetch(sources, mats, loaded)
    serve_body(flag, received, *mats, *old, *outs, *work, ready=ready)


def serve_back_far_body(flag, received, pre_record, *refs):
    sources, refs, mats, loaded = (refs[:3], refs[3:-4], refs[-4:-1], refs[-1])
    old, outs, work = (refs[:2], refs[2:5], refs[8:])
    ready = fetch(sources[::-1], mats[::-1], loaded)
    serve_back_body(flag, received, pre_record, *mats, *old, *outs, *work, ready=ready)


def serve_back_rows(received, load, pre, down_mat, slot_grads, narrow, rows, begin):
    load.start()
    unpack_slots(received, rows)
    slot_grads[...] = rows[...].astype(jnp.bfloat16)
    begin()
    grad_hidden = dot_t(slot_grads[...], down_mat[...])
    load.wait()
    gate = pre[0]
    up = pre[1]
    gate_sig = jax.nn.sigmoid(gate)
    gate_act = gate * gate_sig
    grad_gate = (grad_hidden * up * (gate_sig * (1.0 + gate * (1.0 - gate_sig)))).astype(
        jnp.bfloat16
    )
    grad_up = (grad_hidden * gate_act).astype(jnp.bfloat16)
    inner = gate.shape[1]
    narrow[:, :inner] = (gate_act * up).astype(jnp.bfloat16)
    narrow[:, inner : 2 * inner] = grad_gate
    narrow[:, 2 * inner :] = grad_up
    return (grad_gate, grad_up)


def serve_back_body(
    flag,
    received,
    pre_record,
    gate_mat,
    up_mat,
    down_mat,
    old_grads,
    old_narrow,
    target,
    grads_record,
    narrow_record,
    rows,
    pre,
    slot_grads,
    narrow,
    done,
    ready=lambda index: None,
):
    load = pltpu.make_async_copy(pre_record, pre, done.at[0])
    first = [pltpu.make_async_copy(slot_grads, grads_record, done.at[1])]
    grad_gate, grad_up = serve_back_rows(
        received,
        load,
        pre,
        down_mat,
        slot_grads,
        narrow,
        rows,
        lambda: (keep(flag, first, True), ready(0)),
    )
    ready(1)
    ready(2)
    second = [pltpu.make_async_copy(narrow, narrow_record, done.at[2])]
    keep(flag, second, True)
    rows[...] = dot_t(grad_gate, gate_mat[...]) + dot_t(grad_up, up_mat[...])
    pack_slots(rows, target)
    keep(flag, first + second, False)


def serve_last_body(received, pre_record, down_mat, slot_grads, narrow, rows, pre, done):
    load = pltpu.make_async_copy(pre_record, pre, done.at[0])
    serve_back_rows(received, load, pre, down_mat, slot_grads, narrow, rows, lambda: None)


def lowrank_body(
    flag,
    rows,
    far_in,
    targets,
    head,
    grads,
    far_normed,
    far_act,
    far_pre,
    far_grads,
    far_same,
    mats,
    all_normed,
    all_act,
    all_pre,
    all_grads,
    values,
    inner,
    scale,
    loaded,
    stored,
):
    count = mats.shape[0]
    live = flag[0].astype(jnp.float32)

    def load(index):
        return pltpu.make_async_copy(far_in.at[index], mats.at[index], loaded.at[index])

    def store(kind, index):
        near, far = (
            (all_normed, far_normed),
            (all_act, far_act),
            (all_pre, far_pre),
            (all_grads, far_grads),
        )[kind]
        return pltpu.make_async_copy(near.at[index], far.at[index], stored.at[kind, index])

    for index in reversed(range(count)):
        load(index).start()
    values[0] = rows[...]

    def forward(step, carry):
        index = count - 1 - step
        value = values[step]
        row_scale = rms_scale(value)
        normed = (value.astype(jnp.float32) * row_scale).astype(jnp.bfloat16)
        load(index).wait()
        inner_pre = dot(normed, mats[index, 0])
        act = (inner_pre * jax.nn.sigmoid(inner_pre)).astype(jnp.bfloat16)
        all_normed[index] = normed
        all_act[index] = (act.astype(jnp.float32) * live).astype(jnp.bfloat16)
        store(0, index).start()
        store(1, index).start()
        inner[index] = inner_pre
        scale[index] = row_scale
        values[step + 1] = (
            value.astype(jnp.float32) + dot_t(act, mats[index, 1])
        ).astype(jnp.bfloat16)
        return carry

    lax.fori_loop(0, count, forward, 0)
    final = values[count]
    row_scale = rms_scale(final)
    logits = row_scale * jnp.sum(final.astype(jnp.float32) * head[...], axis=1, keepdims=True)
    grad_logit = jax.nn.sigmoid(logits) - targets[...]
    grads[...] = norm_back(final, row_scale, grad_logit * head[...]).astype(jnp.bfloat16)

    def backward(index, carry):
        value = values[count - 1 - index]
        grad = grads[...]
        inner_pre = inner[index]
        inner_sig = jax.nn.sigmoid(inner_pre)
        grad_act = dot(grad, mats[index, 1])
        grad_pre = (grad_act * (inner_sig * (1.0 + inner_pre * (1.0 - inner_sig)))).astype(
            jnp.bfloat16
        )
        grad_norm = dot_t(grad_pre, mats[index, 0])
        all_pre[index] = (grad_pre.astype(jnp.float32) * live).astype(jnp.bfloat16)
        all_grads[index] = grad
        store(2, index).start()
        store(3, index).start()
        grads[...] = (
            grad.astype(jnp.float32) + norm_back(value, scale[index], grad_norm)
        ).astype(jnp.bfloat16)
        return carry

    lax.fori_loop(0, count, backward, 0)
    for index in range(count):
        for kind in range(4):
            store(kind, index).wait()


def lowrank_layers(flag, rows, mats, targets, head):
    count, rank = (mats.shape[0], mats.shape[3])
    row_count, width = rows.shape
    wide, narrow = ((count, row_count, width), (count, row_count, rank))
    return run_kernel(
        lowrank_body,
        (
            array(rows.shape),
            array(wide),
            array(narrow),
            array(narrow),
            array(wide),
            array(mats.shape),
        ),
        [
            pltpu.VMEM(mats.shape, jnp.bfloat16),
            pltpu.VMEM(wide, jnp.bfloat16),
            pltpu.VMEM(narrow, jnp.bfloat16),
            pltpu.VMEM(narrow, jnp.bfloat16),
            pltpu.VMEM(wide, jnp.bfloat16),
            pltpu.VMEM((count + 1, row_count, width), jnp.bfloat16),
            pltpu.VMEM((count, row_count, rank), jnp.float32),
            pltpu.VMEM((count, row_count, 1), jnp.float32),
            pltpu.SemaphoreType.DMA((count,)),
            pltpu.SemaphoreType.DMA((4, count)),
        ],
        flag,
        rows,
        mats,
        targets,
        head,
        far=(2,),
        far_out=(1, 2, 3, 4, 5),
        scalars=(0,),
        aliases={2: 5},
        limit=40,
    )[:5]


def parts_body(normed, pre, grads, act, parts):
    blocks, _, _, depth, rank = parts.shape
    for kind, (wide, narrow) in enumerate(((normed, pre), (grads, act))):
        part = dot_tn(wide[0], narrow[0]).astype(jnp.bfloat16)
        parts[:, 0, kind] = part.reshape(blocks, depth, rank)


def lowrank_sums(normed, pre, grads, act, blocks):
    count, row_count, width = normed.shape
    rank = pre.shape[2]
    wide = pl.BlockSpec((1, row_count, width), lambda k: (k, 0, 0))
    narrow = pl.BlockSpec((1, row_count, rank), lambda k: (k, 0, 0))
    depth = width // blocks
    return pl.pallas_call(
        parts_body,
        grid=(count,),
        out_shape=pltpu.HBM((blocks, count, 2, depth, rank), jnp.bfloat16),
        in_specs=[wide, narrow, wide, narrow],
        out_specs=pl.BlockSpec((blocks, 1, 2, depth, rank), lambda k: (0, k, 0, 0, 0)),
        compiler_params=pltpu.CompilerParams(vmem_limit_bytes=16 * 1024 * 1024),
        cost_estimate=pl.CostEstimate(
            flops=4 * count * row_count * width * rank,
            bytes_accessed=4 * count * width * (row_count + rank),
            transcendentals=0,
        ),
    )(normed, pre, grads, act)


def weights_body(kept, slot_grads, narrow, gate, up, down):
    inner = gate.shape[1]
    gate[...] = dot_tn(kept[...], narrow[:, inner : 2 * inner])
    up[...] = dot_tn(kept[...], narrow[:, 2 * inner :])
    down[...] = dot_tn(narrow[:, :inner], slot_grads[...])


def weight_sums(kept, slot_grads, narrow):
    slots, width = kept.shape
    inner = narrow.shape[1] // 3
    wide = pl.BlockSpec((slots, inner), lambda k: (0, k))
    tall = pl.BlockSpec((inner, inner), lambda k: (k, 0))
    return pl.pallas_call(
        weights_body,
        grid=(width // inner,),
        out_shape=tuple(
            jax.ShapeDtypeStruct(shape, jnp.float32)
            for shape in ((width, inner), (width, inner), (inner, width))
        ),
        in_specs=[wide, wide, pl.BlockSpec(narrow.shape, lambda k: (0, 0))],
        out_specs=(tall, tall, pl.BlockSpec((inner, inner), lambda k: (0, k))),
    )(kept, slot_grads, narrow)


def exchange(buffer):
    return lax.all_to_all(buffer, "expert", split_axis=0, concat_axis=0, tiled=True)


def work_rows(slots, width):
    return [pltpu.VMEM((slots, width), jnp.float32)]


def packed_shape(table, width):
    count = lax.axis_size("expert")
    return array((count, table.shape[0] // count, width))


def send(values, table):
    width = values.shape[1]
    return run_kernel(
        send_body, packed_shape(table, width), work_rows(table.shape[0], width), values, table
    )


def take(flag, returned, route, values, record):
    table, pick_table, gate = route
    return run_kernel(
        take_body,
        (array(values.shape), array(values.shape)),
        work_rows(table.shape[0], values.shape[1]) + [pltpu.SemaphoreType.DMA((1,))],
        flag,
        returned,
        pick_table,
        values,
        gate,
        record,
        far=(5,),
        far_out=(1,),
        scalars=(0,),
        aliases={5: 1},
    )


def turn(flag, returned, route, values, record, next_table):
    table, pick_table, gate = route
    width = values.shape[1]
    return run_kernel(
        turn_body,
        (array(values.shape), array(values.shape), packed_shape(next_table, width)),
        work_rows(table.shape[0], width) + [pltpu.SemaphoreType.DMA((1,))],
        flag,
        returned,
        pick_table,
        values,
        gate,
        record,
        next_table,
        far=(5,),
        far_out=(1,),
        scalars=(0,),
        aliases={5: 1},
    )


def send_back(grads, route):
    table, _, gate = route
    width = grads.shape[1]
    return run_kernel(
        send_back_body,
        packed_shape(table, width),
        work_rows(table.shape[0], width),
        grads,
        gate,
        table,
    )


def load_rows(slots, values):
    return work_rows(slots, values.shape[1]) + [
        pltpu.VMEM(values.shape, jnp.bfloat16),
        pltpu.SemaphoreType.DMA((1,)),
    ]


def take_back(returned, route, values, grads):
    table, pick_table, _ = route
    return run_kernel(
        take_back_body,
        array(values.shape),
        load_rows(table.shape[0], values),
        returned,
        pick_table,
        values,
        grads,
        far=(2,),
    )


def turn_back(returned, route, values, grads, next_route):
    table, pick_table, _ = route
    return run_kernel(
        turn_back_body,
        (array(values.shape), packed_shape(next_route[0], values.shape[1])),
        load_rows(table.shape[0], values),
        returned,
        pick_table,
        values,
        grads,
        next_route[2],
        next_route[0],
        far=(2,),
    )


def far_mats(mats):
    return [pltpu.VMEM(mat.shape, mat.dtype) for mat in mats] + [pltpu.SemaphoreType.DMA((3,))]


def serve(flag, received, mats, kept, pre, far=False):
    count, depth, width = received.shape
    slots, inner = (count * depth, mats[0].shape[1])
    return run_kernel(
        serve_far_body if far else serve_body,
        (array(received.shape), array((slots, width)), array((2, slots, inner), jnp.float32))
        + (tuple(array(mat.shape) for mat in mats) if far else ()),
        work_rows(slots, width)
        + [
            pltpu.VMEM((slots, width), jnp.bfloat16),
            pltpu.VMEM((2, slots, inner), jnp.float32),
            pltpu.SemaphoreType.DMA((2,)),
        ]
        + (far_mats(mats) if far else []),
        flag,
        received,
        *mats,
        kept,
        pre,
        far=(2, 3, 4, 5, 6) if far else (5, 6),
        far_out=(1, 2, 3, 4, 5),
        scalars=(0,),
        aliases={2: 3, 3: 4, 4: 5, 5: 1, 6: 2} if far else {5: 1, 6: 2},
    )


def serve_back(flag, received, pre, mats, grads, narrow, far=False):
    width = received.shape[2]
    _, slots, inner = pre.shape
    return run_kernel(
        serve_back_far_body if far else serve_back_body,
        (array(received.shape), array((slots, width)), array((slots, 3 * inner)))
        + (tuple(array(mat.shape) for mat in mats) if far else ()),
        work_rows(slots, width)
        + [
            pltpu.VMEM(pre.shape, jnp.float32),
            pltpu.VMEM((slots, width), jnp.bfloat16),
            pltpu.VMEM((slots, 3 * inner), jnp.bfloat16),
            pltpu.SemaphoreType.DMA((3,)),
        ]
        + (far_mats(mats) if far else []),
        flag,
        received,
        pre,
        *mats,
        grads,
        narrow,
        far=(2, 3, 4, 5, 6, 7) if far else (2, 6, 7),
        far_out=(1, 2, 3, 4, 5),
        scalars=(0,),
        aliases={3: 3, 4: 4, 5: 5, 6: 1, 7: 2} if far else {6: 1, 7: 2},
    )


def serve_last(received, pre, down_mat):
    width = received.shape[2]
    _, slots, inner = pre.shape
    return run_kernel(
        serve_last_body,
        (array((slots, width)), array((slots, 3 * inner))),
        work_rows(slots, width)
        + [pltpu.VMEM(pre.shape, jnp.float32), pltpu.SemaphoreType.DMA((1,))],
        received,
        pre,
        down_mat,
        far=(1,),
    )


def local(
    features,
    labels,
    routes,
    route_gates,
    gate_weight,
    up_weight,
    down_weight,
    lowrank_in,
    lowrank_out,
    head_weight,
):
    section_count = lax.axis_size("section")
    section = lax.axis_index("section")
    expert_count = lax.axis_size("expert")
    micro_count, row_count, width = features.shape
    is_even = section % 2 == 0
    pair = section // 2
    to_odd = [(s, s + 1) for s in range(0, section_count, 2)]
    to_even = [(s + 1, s) for s in range(0, section_count, 2)]

    def swap(value):
        return lax.ppermute(value, "section", to_odd + to_even)

    def hop(value, layer):
        first = 0 if layer % 4 < 2 else 2
        links = []
        for start in range(first, first + section_count, 4):
            for lower in (start, start + 1):
                low_end, high_end = (lower % section_count, (lower + 2) % section_count)
                links += [(low_end, high_end), (high_end, low_end)]
        half = value.shape[0] // 2
        parts = [lax.ppermute(part, "section", links) for part in (value[:half], value[half:])]
        return jnp.concatenate(parts, axis=0)

    own = (gate_weight[0, 0], up_weight[0, 0], down_weight[0, 0])
    gate_other, up_other = (swap(own[0]), swap(own[1]))

    ids = routes[0, :, :, 0]
    plan = jnp.concatenate([ids.astype(jnp.float32), route_gates[0]], axis=0)
    plan_other = swap(plan)

    def route_of(slots, slot_count, gates):
        table = table_of(slots, slot_count)
        grid = jnp.arange(slot_count, dtype=jnp.int32)
        pick_table = (slots[:, None] == grid[None, :]).astype(jnp.bfloat16)
        return (table, pick_table, gates[:, None])

    def pick(first, second):
        chosen = jnp.where(is_even, first, second)
        mine = jnp.where(is_even, chosen[0::2], chosen[1::2])
        slots = slot_of_rows(mine[0].astype(jnp.int32), expert_count, capacity, 0)
        return route_of(slots, expert_count * capacity, mine[1])

    route_even = pick(plan, plan_other)
    route_odd = pick(plan_other, plan)
    joint_slots = jnp.concatenate(
        [
            slot_of_rows(ids[m], expert_count, capacity * micro_count, capacity * m)
            for m in range(micro_count)
        ]
    )
    route_all = route_of(
        joint_slots, expert_count * capacity * micro_count, route_gates[0].reshape(-1)
    )
    routing = [route_odd if layer % 2 else route_even for layer in range(section_count)]

    flags = [(pair == layer // 2).astype(jnp.int32)[None] for layer in range(section_count)]
    always = jnp.ones((1,), jnp.int32)
    first_rows = features.reshape(-1, width)
    served, kept_all, pre_all = serve(
        always, exchange(send(first_rows, route_all[0])), own, None, None
    )
    second_rows, _ = take(always, exchange(served), route_all, first_rows, None)
    second_rows, late = lax.optimization_barrier((second_rows, own[2]))
    crossing = lax.ppermute(second_rows[row_count:], "section", to_odd)
    down_back = lax.ppermute(late, "section", to_even)
    rows = jnp.where(is_even, second_rows[:row_count], crossing)
    rows, late = lax.optimization_barrier((rows, own[2]))
    down_on = lax.ppermute(late, "section", to_odd)
    sending = send(rows, routing[1][0])
    sending, gate_other, up_other = lax.optimization_barrier((sending, gate_other, up_other))
    others = (gate_other, up_other)
    mats_odd = tuple(jnp.where(is_even, b, a) for a, b in zip(own, others + (down_back,)))

    row_record = [None, None]
    kept_record = [None, None]
    pre_record = [None, None]
    for layer in range(1, section_count):
        side = layer % 2
        served, kept_record[side], pre_record[side], *moved = serve(
            flags[layer],
            exchange(sending),
            mats_odd if side else mats_even,
            kept_record[side],
            pre_record[side],
            far=side == 0,
        )
        if side == 0:
            mats_even = moved
        returned = exchange(served)
        if side == 0:
            rows, row_record[side], sending = turn(
                flags[layer],
                returned,
                routing[layer],
                rows,
                row_record[side],
                routing[layer + 1][0],
            )
            if layer == 2:
                low_own = jnp.stack([lowrank_in[0], lowrank_out[0].T])
                low_own, rows = lax.optimization_barrier((low_own, rows))
                low_mats = lax.all_gather(low_own, "section")
        else:
            rows, row_record[side] = take(
                flags[layer], returned, routing[layer], rows, row_record[side]
            )
            if layer == 1:
                rows, down_on = lax.optimization_barrier((rows, down_on))
                on = others + (down_on,)
                mats_even = tuple(jnp.where(is_even, a, b) for a, b in zip(own, on))
            if layer < section_count - 1:
                rows = hop(rows, layer)
                sending = send(rows, routing[layer + 1][0])

    targets = jnp.where(is_even, labels[0], labels[1]).astype(jnp.float32)[:, None]
    grads, low_normed, low_act, low_pre, low_grads = lowrank_layers(
        flags[-1], rows, low_mats, targets, head_weight[None, :]
    )
    sending = send_back(grads, routing[section_count - 1])
    sending, low_normed, low_act, low_pre, low_grads = lax.optimization_barrier(
        (sending, low_normed, low_act, low_pre, low_grads)
    )

    parts = lowrank_sums(low_normed, low_pre, low_grads, low_act, expert_count)
    last_pair = section_count // 2 - 1

    grads_record = [None, None]
    narrow_record = [None, None]
    for layer in reversed(range(1, section_count)):
        side = layer % 2
        target, grads_record[side], narrow_record[side], *moved = serve_back(
            flags[layer],
            exchange(sending),
            pre_record[side],
            mats_odd if side else mats_even,
            grads_record[side],
            narrow_record[side],
            far=side == 0,
        )
        mats_even = moved if side == 0 else mats_even
        returned = exchange(target)
        values = row_record[side]
        if side == 1 and layer > 1:
            grads, sending = turn_back(returned, routing[layer], values, grads, routing[layer - 1])
        else:
            grads = take_back(returned, routing[layer], values, grads)
        if layer == section_count - 1:
            parts, sending = lax.optimization_barrier((parts, sending))
            share = lax.psum_scatter(
                parts.reshape(-1, parts.shape[-1]), "expert", scatter_dimension=0, tiled=True
            ).reshape(parts.shape[1:])
        if layer == 2:
            share, grads = lax.optimization_barrier((share, grads))
            share = lax.all_to_all(share, "section", split_axis=0, concat_axis=0, tiled=True)
        if layer % 2 == 0:
            grads = hop(grads, layer - 2)
            sending = send_back(grads, routing[layer - 1])

    all_grads = jnp.concatenate([grads, lax.ppermute(grads, "section", to_even)], axis=0)
    saved = tuple(zip(kept_record, grads_record, narrow_record))
    theirs = tuple(swap(jnp.where(is_even, b, a)) for a, b in zip(*saved))
    held = tuple(jnp.where(is_even, a, b) for a, b in zip(*saved))
    joint = (kept_all,) + tuple(
        serve_last(exchange(send_back(all_grads, route_all)), pre_all, own[2])
    )
    kept, slot_grads, narrow = (
        jnp.where(section == 0, both, jnp.concatenate([mine, other], axis=0))
        for both, mine, other in zip(joint, held, theirs)
    )
    sums = weight_sums(kept, slot_grads, narrow)
    share = jnp.sum(share[2 * last_pair :].astype(jnp.float32), axis=0)
    return (
        sums[0][None, None],
        sums[1][None, None],
        sums[2][None, None],
        share[0][None],
        share[1].T[None],
    )


def solution(mesh):
    return jax.shard_map(
        local,
        mesh=mesh,
        in_specs=(
            P(None, "expert", None),
            P(None, "expert"),
            P("section", None, "expert", None),
            P("section", None, "expert"),
            P("section", "expert", None, None),
            P("section", "expert", None, None),
            P("section", "expert", None, None),
            P("section", None, None),
            P("section", None, None),
            P(),
        ),
        out_specs=(
            P("section", "expert", None, None),
            P("section", "expert", None, None),
            P("section", "expert", None, None),
            P("section", "expert", None),
            P("section", None, "expert"),
        ),
        check_vma=False,
    )
```

```python
import jax
import jax.numpy as jnp
from jax import lax
from jax.experimental import pallas as pl
from jax.experimental.pallas import tpu as pltpu
from jax.sharding import PartitionSpec as P

epsilon = 1e-06
capacity = 3


def dot(left, right):
    return jnp.dot(left, right, preferred_element_type=jnp.float32)


def dot_t(left, right):
    return lax.dot_general(left, right, (((1,), (1,)), ((), ())), preferred_element_type=jnp.float32)


def dot_tn(left, right):
    return lax.dot_general(left, right, (((0,), (0,)), ((), ())), preferred_element_type=jnp.float32)


def rms_scale(values):
    widened = values.astype(jnp.float32)
    return lax.rsqrt(jnp.mean(widened * widened, axis=-1, keepdims=True) + epsilon)


def norm_back(values, row_scale, grad_norm):
    widened = values.astype(jnp.float32)
    inner_mean = jnp.mean(grad_norm * widened, axis=-1, keepdims=True)
    return row_scale * grad_norm - widened * (row_scale * row_scale * row_scale) * inner_mean


def slot_of_rows(expert_ids, expert_count, stride, offset):
    chosen = (expert_ids[:, None] == jnp.arange(expert_count, dtype=jnp.int32)[None, :]).astype(
        jnp.int32
    )
    earlier = jnp.arange(expert_ids.shape[0])[:, None] > jnp.arange(expert_ids.shape[0])[None, :]
    same = expert_ids[:, None] == expert_ids[None, :]
    rank = jnp.sum((same & earlier).astype(jnp.int32), axis=1)
    return expert_ids * stride + offset + rank


def table_of(slots, slot_count):
    grid = jnp.arange(slot_count, dtype=jnp.int32)
    return (grid[:, None] == slots[None, :]).astype(jnp.bfloat16)


def run_kernel(
    body, out_shape, scratch, *operands, far=(), far_out=(), scalars=(), aliases={}, limit=16
):
    absent = [k for k, operand in enumerate(operands) if operand is None]
    if absent:
        count, inner_body = (len(operands), body)
        operands = [operand for operand in operands if operand is not None]
        shift = {
            k: k - sum(gone < k for gone in absent) for k in range(count) if k not in absent
        }
        far, scalars = (tuple(shift[k] for k in group if k in shift) for group in (far, scalars))
        aliases = {shift[k]: out for k, out in aliases.items() if k in shift}

        def body(*refs):
            refs = iter(refs)
            given = [None if k in absent else next(refs) for k in range(count)]
            inner_body(*given, *refs)

    everywhere = pl.BlockSpec(memory_space=pltpu.HBM)
    near = pl.BlockSpec(memory_space=pltpu.VMEM)
    small = pl.BlockSpec(memory_space=pltpu.SMEM)
    in_specs = [
        small if k in scalars else everywhere if k in far else near for k in range(len(operands))
    ]
    leaves, treedef = jax.tree.flatten(out_shape)
    leaves = [
        pltpu.HBM(leaf.shape, leaf.dtype) if k in far_out else leaf
        for k, leaf in enumerate(leaves)
    ]
    out_specs = [everywhere if k in far_out else near for k in range(len(leaves))]
    return pl.pallas_call(
        body,
        out_shape=jax.tree.unflatten(treedef, leaves),
        in_specs=in_specs,
        out_specs=jax.tree.unflatten(treedef, out_specs),
        scratch_shapes=scratch,
        input_output_aliases=aliases,
        compiler_params=pltpu.CompilerParams(vmem_limit_bytes=limit * 1024 * 1024),
    )(*operands)


def array(shape, dtype=jnp.bfloat16):
    return jax.ShapeDtypeStruct(shape, dtype)


def unpack_slots(source, rows):
    count, depth, _ = source.shape
    for index in range(count):
        rows[depth * index : depth * (index + 1), :] = source[index].astype(jnp.float32)


def pack_slots(rows, target):
    count, depth, _ = target.shape
    for index in range(count):
        target[index] = rows[depth * index : depth * (index + 1), :].astype(jnp.bfloat16)


def normed_rows(values):
    widened = values.astype(jnp.float32)
    return (widened * rms_scale(values)).astype(jnp.bfloat16)


def send_body(values, table, target, rows):
    rows[...] = dot(table[...], normed_rows(values[...]))
    pack_slots(rows, target)


def take_rows(returned, pick_table, values, gate, result, rows):
    unpack_slots(returned, rows)
    gathered = dot(pick_table[...], rows[...].astype(jnp.bfloat16))
    result[...] = (values[...].astype(jnp.float32) + gate[...] * gathered).astype(jnp.bfloat16)


def keep(flag, copies, begin):
    @pl.when(flag[0] == 1)
    def _():
        for copy in copies:
            copy.start() if begin else copy.wait()


def take_body(flag, returned, pick_table, values, gate, old, result, record, rows, done):
    copies = [pltpu.make_async_copy(values, record, done.at[0])]
    keep(flag, copies, True)
    take_rows(returned, pick_table, values, gate, result, rows)
    keep(flag, copies, False)


def turn_body(
    flag, returned, pick_table, values, gate, old, table, result, record, target, rows, done
):
    copies = [pltpu.make_async_copy(values, record, done.at[0])]
    keep(flag, copies, True)
    take_rows(returned, pick_table, values, gate, result, rows)
    send_body(result, table, target, rows)
    keep(flag, copies, False)


def send_back_body(grads, gate, table, target, rows):
    grad_out = (gate[...] * grads[...].astype(jnp.float32)).astype(jnp.bfloat16)
    rows[...] = dot(table[...], grad_out)
    pack_slots(rows, target)


def take_back_body(returned, pick_table, record, grads, result, rows, values, done):
    load = pltpu.make_async_copy(record, values, done.at[0])
    load.start()
    unpack_slots(returned, rows)
    grad_norm = dot(pick_table[...], rows[...].astype(jnp.bfloat16))
    load.wait()
    value = values[...]
    result[...] = (
        grads[...].astype(jnp.float32) + norm_back(value, rms_scale(value), grad_norm)
    ).astype(jnp.bfloat16)


def turn_back_body(
    returned, pick_table, record, grads, gate, table, result, target, rows, values, done
):
    take_back_body(returned, pick_table, record, grads, result, rows, values, done)
    send_back_body(result, gate, table, target, rows)


def serve_body(
    flag,
    received,
    gate_mat,
    up_mat,
    down_mat,
    old_kept,
    old_pre,
    served,
    kept_record,
    pre_record,
    rows,
    kept,
    pre,
    done,
    ready=lambda index: None,
):
    unpack_slots(received, rows)
    kept[...] = rows[...].astype(jnp.bfloat16)
    first = [pltpu.make_async_copy(kept, kept_record, done.at[0])]
    keep(flag, first, True)
    ready(0)
    pre[0] = dot(kept[...], gate_mat[...])
    ready(1)
    pre[1] = dot(kept[...], up_mat[...])
    second = [pltpu.make_async_copy(pre, pre_record, done.at[1])]
    keep(flag, second, True)
    gate = pre[0]
    hidden = (gate * jax.nn.sigmoid(gate) * pre[1]).astype(jnp.bfloat16)
    ready(2)
    rows[...] = dot(hidden, down_mat[...])
    pack_slots(rows, served)
    keep(flag, first + second, False)


def fetch(sources, targets, done):
    copies = [
        pltpu.make_async_copy(source, target, done.at[index])
        for index, (source, target) in enumerate(zip(sources, targets))
    ]
    for copy in copies:
        copy.start()
    return lambda index: copies[index].wait()


def serve_far_body(flag, received, *refs):
    sources, refs, mats, loaded = (refs[:3], refs[3:-4], refs[-4:-1], refs[-1])
    old, outs, work = (refs[:2], refs[2:5], refs[8:])
    ready = fetch(sources, mats, loaded)
    serve_body(flag, received, *mats, *old, *outs, *work, ready=ready)


def serve_back_far_body(flag, received, pre_record, *refs):
    sources, refs, mats, loaded = (refs[:3], refs[3:-4], refs[-4:-1], refs[-1])
    old, outs, work = (refs[:2], refs[2:5], refs[8:])
    ready = fetch(sources[::-1], mats[::-1], loaded)
    serve_back_body(flag, received, pre_record, *mats, *old, *outs, *work, ready=ready)


def serve_back_rows(received, load, pre, down_mat, slot_grads, narrow, rows, begin):
    load.start()
    unpack_slots(received, rows)
    slot_grads[...] = rows[...].astype(jnp.bfloat16)
    begin()
    grad_hidden = dot_t(slot_grads[...], down_mat[...])
    load.wait()
    gate = pre[0]
    up = pre[1]
    gate_sig = jax.nn.sigmoid(gate)
    gate_act = gate * gate_sig
    grad_gate = (grad_hidden * up * (gate_sig * (1.0 + gate * (1.0 - gate_sig)))).astype(
        jnp.bfloat16
    )
    grad_up = (grad_hidden * gate_act).astype(jnp.bfloat16)
    inner = gate.shape[1]
    narrow[:, :inner] = (gate_act * up).astype(jnp.bfloat16)
    narrow[:, inner : 2 * inner] = grad_gate
    narrow[:, 2 * inner :] = grad_up
    return (grad_gate, grad_up)


def serve_back_body(
    flag,
    received,
    pre_record,
    gate_mat,
    up_mat,
    down_mat,
    old_grads,
    old_narrow,
    target,
    grads_record,
    narrow_record,
    rows,
    pre,
    slot_grads,
    narrow,
    done,
    ready=lambda index: None,
):
    load = pltpu.make_async_copy(pre_record, pre, done.at[0])
    first = [pltpu.make_async_copy(slot_grads, grads_record, done.at[1])]
    grad_gate, grad_up = serve_back_rows(
        received,
        load,
        pre,
        down_mat,
        slot_grads,
        narrow,
        rows,
        lambda: (keep(flag, first, True), ready(0)),
    )
    ready(1)
    ready(2)
    second = [pltpu.make_async_copy(narrow, narrow_record, done.at[2])]
    keep(flag, second, True)
    rows[...] = dot_t(grad_gate, gate_mat[...]) + dot_t(grad_up, up_mat[...])
    pack_slots(rows, target)
    keep(flag, first + second, False)


def serve_last_body(received, pre_record, down_mat, slot_grads, narrow, rows, pre, done):
    load = pltpu.make_async_copy(pre_record, pre, done.at[0])
    serve_back_rows(received, load, pre, down_mat, slot_grads, narrow, rows, lambda: None)


def lowrank_body(
    flag,
    rows,
    far_in,
    targets,
    head,
    grads,
    far_normed,
    far_act,
    far_pre,
    far_grads,
    far_same,
    mats,
    all_normed,
    all_act,
    all_pre,
    all_grads,
    values,
    inner,
    scale,
    loaded,
    stored,
):
    count = mats.shape[0]
    live = flag[0].astype(jnp.float32)

    def load(index):
        return pltpu.make_async_copy(far_in.at[index], mats.at[index], loaded.at[index])

    def store(kind, index):
        near, far = (
            (all_normed, far_normed),
            (all_act, far_act),
            (all_pre, far_pre),
            (all_grads, far_grads),
        )[kind]
        return pltpu.make_async_copy(near.at[index], far.at[index], stored.at[kind, index])

    for index in reversed(range(count)):
        load(index).start()
    values[0] = rows[...]

    def forward(step, carry):
        index = count - 1 - step
        value = values[step]
        row_scale = rms_scale(value)
        normed = (value.astype(jnp.float32) * row_scale).astype(jnp.bfloat16)
        load(index).wait()
        inner_pre = dot(normed, mats[index, 0])
        act = (inner_pre * jax.nn.sigmoid(inner_pre)).astype(jnp.bfloat16)
        all_normed[index] = normed
        all_act[index] = (act.astype(jnp.float32) * live).astype(jnp.bfloat16)
        store(0, index).start()
        store(1, index).start()
        inner[index] = inner_pre
        scale[index] = row_scale
        values[step + 1] = (
            value.astype(jnp.float32) + dot_t(act, mats[index, 1])
        ).astype(jnp.bfloat16)
        return carry

    lax.fori_loop(0, count, forward, 0)
    final = values[count]
    row_scale = rms_scale(final)
    logits = row_scale * jnp.sum(final.astype(jnp.float32) * head[...], axis=1, keepdims=True)
    grad_logit = jax.nn.sigmoid(logits) - targets[...]
    grads[...] = norm_back(final, row_scale, grad_logit * head[...]).astype(jnp.bfloat16)

    def backward(index, carry):
        value = values[count - 1 - index]
        grad = grads[...]
        inner_pre = inner[index]
        inner_sig = jax.nn.sigmoid(inner_pre)
        grad_act = dot(grad, mats[index, 1])
        grad_pre = (grad_act * (inner_sig * (1.0 + inner_pre * (1.0 - inner_sig)))).astype(
            jnp.bfloat16
        )
        grad_norm = dot_t(grad_pre, mats[index, 0])
        all_pre[index] = (grad_pre.astype(jnp.float32) * live).astype(jnp.bfloat16)
        all_grads[index] = grad
        store(2, index).start()
        store(3, index).start()
        grads[...] = (
            grad.astype(jnp.float32) + norm_back(value, scale[index], grad_norm)
        ).astype(jnp.bfloat16)
        return carry

    lax.fori_loop(0, count, backward, 0)
    for index in range(count):
        for kind in range(4):
            store(kind, index).wait()


def lowrank_layers(flag, rows, mats, targets, head):
    count, rank = (mats.shape[0], mats.shape[3])
    row_count, width = rows.shape
    wide, narrow = ((count, row_count, width), (count, row_count, rank))
    return run_kernel(
        lowrank_body,
        (
            array(rows.shape),
            array(wide),
            array(narrow),
            array(narrow),
            array(wide),
            array(mats.shape),
        ),
        [
            pltpu.VMEM(mats.shape, jnp.bfloat16),
            pltpu.VMEM(wide, jnp.bfloat16),
            pltpu.VMEM(narrow, jnp.bfloat16),
            pltpu.VMEM(narrow, jnp.bfloat16),
            pltpu.VMEM(wide, jnp.bfloat16),
            pltpu.VMEM((count + 1, row_count, width), jnp.bfloat16),
            pltpu.VMEM((count, row_count, rank), jnp.float32),
            pltpu.VMEM((count, row_count, 1), jnp.float32),
            pltpu.SemaphoreType.DMA((count,)),
            pltpu.SemaphoreType.DMA((4, count)),
        ],
        flag,
        rows,
        mats,
        targets,
        head,
        far=(2,),
        far_out=(1, 2, 3, 4, 5),
        scalars=(0,),
        aliases={2: 5},
        limit=40,
    )[:5]


def parts_body(normed, pre, grads, act, parts):
    blocks, _, _, depth, rank = parts.shape
    for kind, (wide, narrow) in enumerate(((normed, pre), (grads, act))):
        part = dot_tn(wide[0], narrow[0]).astype(jnp.bfloat16)
        parts[:, 0, kind] = part.reshape(blocks, depth, rank)


def lowrank_sums(normed, pre, grads, act, blocks):
    count, row_count, width = normed.shape
    rank = pre.shape[2]
    wide = pl.BlockSpec((1, row_count, width), lambda k: (k, 0, 0))
    narrow = pl.BlockSpec((1, row_count, rank), lambda k: (k, 0, 0))
    depth = width // blocks
    return pl.pallas_call(
        parts_body,
        grid=(count,),
        out_shape=pltpu.HBM((blocks, count, 2, depth, rank), jnp.bfloat16),
        in_specs=[wide, narrow, wide, narrow],
        out_specs=pl.BlockSpec((blocks, 1, 2, depth, rank), lambda k: (0, k, 0, 0, 0)),
        compiler_params=pltpu.CompilerParams(vmem_limit_bytes=16 * 1024 * 1024),
        cost_estimate=pl.CostEstimate(
            flops=4 * count * row_count * width * rank,
            bytes_accessed=4 * count * width * (row_count + rank),
            transcendentals=0,
        ),
    )(normed, pre, grads, act)


def choose(flag, joint, mine, theirs, chosen):
    half = mine.shape[0]

    @pl.when(flag[0] == 1)
    def _():
        chosen[...] = joint[...]

    @pl.when(flag[0] != 1)
    def _():
        chosen[:half, :] = mine[...]
        chosen[half:, :] = theirs[...]


def weights_body(flag, *refs):
    sources, (gate, up, down), (kept, slot_grads, narrow) = (refs[:9], refs[9:12], refs[12:])
    choose(flag, *sources[0:3], kept)
    choose(flag, *sources[3:6], slot_grads)

    @pl.when(pl.program_id(0) == 0)
    def _():
        choose(flag, *sources[6:9], narrow)

    inner = gate.shape[1]
    gate[...] = dot_tn(kept[...], narrow[:, inner : 2 * inner])
    up[...] = dot_tn(kept[...], narrow[:, 2 * inner :])
    down[...] = dot_tn(narrow[:, :inner], slot_grads[...])


def weight_sums(flag, *triples):
    slots, width = triples[0][0].shape
    inner = triples[2][0].shape[1] // 3
    block = 2 * inner
    in_specs = [pl.BlockSpec(memory_space=pltpu.SMEM)]
    for triple in triples[:2]:
        in_specs += [pl.BlockSpec((part.shape[0], block), lambda k: (0, k)) for part in triple]
    in_specs += [pl.BlockSpec(part.shape, lambda k: (0, 0)) for part in triples[2]]
    tall = pl.BlockSpec((block, inner), lambda k: (k, 0))
    return pl.pallas_call(
        weights_body,
        grid=(width // block,),
        out_shape=tuple(
            jax.ShapeDtypeStruct(shape, jnp.float32)
            for shape in ((width, inner), (width, inner), (inner, width))
        ),
        in_specs=in_specs,
        out_specs=(tall, tall, pl.BlockSpec((inner, block), lambda k: (0, k))),
        scratch_shapes=[
            pltpu.VMEM((slots, block), jnp.bfloat16),
            pltpu.VMEM((slots, block), jnp.bfloat16),
            pltpu.VMEM((slots, 3 * inner), jnp.bfloat16),
        ],
        compiler_params=pltpu.CompilerParams(vmem_limit_bytes=16 * 1024 * 1024),
    )(flag, *(part for triple in triples for part in triple))


def exchange(buffer):
    return lax.all_to_all(buffer, "expert", split_axis=0, concat_axis=0, tiled=True)


def work_rows(slots, width):
    return [pltpu.VMEM((slots, width), jnp.float32)]


def packed_shape(table, width):
    count = lax.axis_size("expert")
    return array((count, table.shape[0] // count, width))


def send(values, table):
    width = values.shape[1]
    return run_kernel(
        send_body, packed_shape(table, width), work_rows(table.shape[0], width), values, table
    )


def take(flag, returned, route, values, record):
    table, pick_table, gate = route
    return run_kernel(
        take_body,
        (array(values.shape), array(values.shape)),
        work_rows(table.shape[0], values.shape[1]) + [pltpu.SemaphoreType.DMA((1,))],
        flag,
        returned,
        pick_table,
        values,
        gate,
        record,
        far=(5,),
        far_out=(1,),
        scalars=(0,),
        aliases={5: 1},
    )


def turn(flag, returned, route, values, record, next_table):
    table, pick_table, gate = route
    width = values.shape[1]
    return run_kernel(
        turn_body,
        (array(values.shape), array(values.shape), packed_shape(next_table, width)),
        work_rows(table.shape[0], width) + [pltpu.SemaphoreType.DMA((1,))],
        flag,
        returned,
        pick_table,
        values,
        gate,
        record,
        next_table,
        far=(5,),
        far_out=(1,),
        scalars=(0,),
        aliases={5: 1},
    )


def send_back(grads, route):
    table, _, gate = route
    width = grads.shape[1]
    return run_kernel(
        send_back_body,
        packed_shape(table, width),
        work_rows(table.shape[0], width),
        grads,
        gate,
        table,
    )


def load_rows(slots, values):
    return work_rows(slots, values.shape[1]) + [
        pltpu.VMEM(values.shape, jnp.bfloat16),
        pltpu.SemaphoreType.DMA((1,)),
    ]


def take_back(returned, route, values, grads):
    table, pick_table, _ = route
    return run_kernel(
        take_back_body,
        array(values.shape),
        load_rows(table.shape[0], values),
        returned,
        pick_table,
        values,
        grads,
        far=(2,),
    )


def turn_back(returned, route, values, grads, next_route):
    table, pick_table, _ = route
    return run_kernel(
        turn_back_body,
        (array(values.shape), packed_shape(next_route[0], values.shape[1])),
        load_rows(table.shape[0], values),
        returned,
        pick_table,
        values,
        grads,
        next_route[2],
        next_route[0],
        far=(2,),
    )


def far_mats(mats):
    return [pltpu.VMEM(mat.shape, mat.dtype) for mat in mats] + [pltpu.SemaphoreType.DMA((3,))]


def serve(flag, received, mats, kept, pre, far=False):
    count, depth, width = received.shape
    slots, inner = (count * depth, mats[0].shape[1])
    return run_kernel(
        serve_far_body if far else serve_body,
        (array(received.shape), array((slots, width)), array((2, slots, inner), jnp.float32))
        + (tuple(array(mat.shape) for mat in mats) if far else ()),
        work_rows(slots, width)
        + [
            pltpu.VMEM((slots, width), jnp.bfloat16),
            pltpu.VMEM((2, slots, inner), jnp.float32),
            pltpu.SemaphoreType.DMA((2,)),
        ]
        + (far_mats(mats) if far else []),
        flag,
        received,
        *mats,
        kept,
        pre,
        far=(2, 3, 4, 5, 6) if far else (5, 6),
        far_out=(1, 2, 3, 4, 5),
        scalars=(0,),
        aliases={2: 3, 3: 4, 4: 5, 5: 1, 6: 2} if far else {5: 1, 6: 2},
    )


def serve_back(flag, received, pre, mats, grads, narrow, far=False):
    width = received.shape[2]
    _, slots, inner = pre.shape
    return run_kernel(
        serve_back_far_body if far else serve_back_body,
        (array(received.shape), array((slots, width)), array((slots, 3 * inner)))
        + (tuple(array(mat.shape) for mat in mats) if far else ()),
        work_rows(slots, width)
        + [
            pltpu.VMEM(pre.shape, jnp.float32),
            pltpu.VMEM((slots, width), jnp.bfloat16),
            pltpu.VMEM((slots, 3 * inner), jnp.bfloat16),
            pltpu.SemaphoreType.DMA((3,)),
        ]
        + (far_mats(mats) if far else []),
        flag,
        received,
        pre,
        *mats,
        grads,
        narrow,
        far=(2, 3, 4, 5, 6, 7) if far else (2, 6, 7),
        far_out=(1, 2, 3, 4, 5),
        scalars=(0,),
        aliases={3: 3, 4: 4, 5: 5, 6: 1, 7: 2} if far else {6: 1, 7: 2},
    )


def serve_last(received, pre, down_mat):
    width = received.shape[2]
    _, slots, inner = pre.shape
    return run_kernel(
        serve_last_body,
        (array((slots, width)), array((slots, 3 * inner))),
        work_rows(slots, width)
        + [pltpu.VMEM(pre.shape, jnp.float32), pltpu.SemaphoreType.DMA((1,))],
        received,
        pre,
        down_mat,
        far=(1,),
    )


def local(
    features,
    labels,
    routes,
    route_gates,
    gate_weight,
    up_weight,
    down_weight,
    lowrank_in,
    lowrank_out,
    head_weight,
):
    section_count = lax.axis_size("section")
    section = lax.axis_index("section")
    expert_count = lax.axis_size("expert")
    micro_count, row_count, width = features.shape
    is_even = section % 2 == 0
    pair = section // 2
    to_odd = [(s, s + 1) for s in range(0, section_count, 2)]
    to_even = [(s + 1, s) for s in range(0, section_count, 2)]

    def swap(value):
        return lax.ppermute(value, "section", to_odd + to_even)

    def hop(value, layer):
        first = 0 if layer % 4 < 2 else 2
        links = []
        for start in range(first, first + section_count, 4):
            for lower in (start, start + 1):
                low_end, high_end = (lower % section_count, (lower + 2) % section_count)
                links += [(low_end, high_end), (high_end, low_end)]
        half = value.shape[0] // 2
        parts = [lax.ppermute(part, "section", links) for part in (value[:half], value[half:])]
        return jnp.concatenate(parts, axis=0)

    own = (gate_weight[0, 0], up_weight[0, 0], down_weight[0, 0])
    gate_other, up_other = (swap(own[0]), swap(own[1]))

    ids = routes[0, :, :, 0]
    plan = jnp.concatenate([ids.astype(jnp.float32), route_gates[0]], axis=0)
    plan_other = swap(plan)

    def route_of(slots, slot_count, gates):
        table = table_of(slots, slot_count)
        grid = jnp.arange(slot_count, dtype=jnp.int32)
        pick_table = (slots[:, None] == grid[None, :]).astype(jnp.bfloat16)
        return (table, pick_table, gates[:, None])

    def pick(first, second):
        chosen = jnp.where(is_even, first, second)
        mine = jnp.where(is_even, chosen[0::2], chosen[1::2])
        slots = slot_of_rows(mine[0].astype(jnp.int32), expert_count, capacity, 0)
        return route_of(slots, expert_count * capacity, mine[1])

    route_even = pick(plan, plan_other)
    route_odd = pick(plan_other, plan)
    joint_slots = jnp.concatenate(
        [
            slot_of_rows(ids[m], expert_count, capacity * micro_count, capacity * m)
            for m in range(micro_count)
        ]
    )
    route_all = route_of(
        joint_slots, expert_count * capacity * micro_count, route_gates[0].reshape(-1)
    )

    flags = [(pair == layer // 2).astype(jnp.int32)[None] for layer in range(section_count)]
    always = jnp.ones((1,), jnp.int32)
    first_rows = features.reshape(-1, width)
    served, kept_all, pre_all = serve(
        always, exchange(send(first_rows, route_all[0])), own, None, None
    )
    targets = jnp.where(is_even, labels[0], labels[1]).astype(jnp.float32)[:, None]
    on_first = (section == 0).astype(jnp.int32)[None]
    served, route_all, route_even, route_odd, flags, targets, on_first = lax.optimization_barrier(
        (served, route_all, route_even, route_odd, flags, targets, on_first)
    )
    routing = [route_odd if layer % 2 else route_even for layer in range(section_count)]
    second_rows, _ = take(always, exchange(served), route_all, first_rows, None)
    second_rows, late = lax.optimization_barrier((second_rows, own[2]))
    crossing = lax.ppermute(second_rows[row_count:], "section", to_odd)
    down_back = lax.ppermute(late, "section", to_even)
    rows = jnp.where(is_even, second_rows[:row_count], crossing)
    rows, late = lax.optimization_barrier((rows, own[2]))
    down_on = lax.ppermute(late, "section", to_odd)
    sending = send(rows, routing[1][0])
    sending, gate_other, up_other = lax.optimization_barrier((sending, gate_other, up_other))
    others = (gate_other, up_other)
    mats_odd = tuple(jnp.where(is_even, b, a) for a, b in zip(own, others + (down_back,)))

    row_record = [None, None]
    kept_record = [None, None]
    pre_record = [None, None]
    for layer in range(1, section_count):
        side = layer % 2
        served, kept_record[side], pre_record[side], *moved = serve(
            flags[layer],
            exchange(sending),
            mats_odd if side else mats_even,
            kept_record[side],
            pre_record[side],
            far=side == 0,
        )
        if side == 0:
            mats_even = moved
        returned = exchange(served)
        if side == 0:
            rows, row_record[side], sending = turn(
                flags[layer],
                returned,
                routing[layer],
                rows,
                row_record[side],
                routing[layer + 1][0],
            )
            if layer == 2:
                low_own = jnp.stack([lowrank_in[0], lowrank_out[0].T])
                low_own, rows = lax.optimization_barrier((low_own, rows))
                low_mats = lax.all_gather(low_own, "section")
        else:
            rows, row_record[side] = take(
                flags[layer], returned, routing[layer], rows, row_record[side]
            )
            if layer == 1:
                rows, down_on = lax.optimization_barrier((rows, down_on))
                on = others + (down_on,)
                mats_even = tuple(jnp.where(is_even, a, b) for a, b in zip(own, on))
            if layer < section_count - 1:
                rows = hop(rows, layer)
                sending = send(rows, routing[layer + 1][0])

    grads, low_normed, low_act, low_pre, low_grads = lowrank_layers(
        flags[-1], rows, low_mats, targets, head_weight[None, :]
    )
    sending = send_back(grads, routing[section_count - 1])
    sending, low_normed, low_act, low_pre, low_grads = lax.optimization_barrier(
        (sending, low_normed, low_act, low_pre, low_grads)
    )

    parts = lowrank_sums(low_normed, low_pre, low_grads, low_act, expert_count)
    last_pair = section_count // 2 - 1

    grads_record = [None, None]
    narrow_record = [None, None]
    for layer in reversed(range(1, section_count)):
        side = layer % 2
        target, grads_record[side], narrow_record[side], *moved = serve_back(
            flags[layer],
            exchange(sending),
            pre_record[side],
            mats_odd if side else mats_even,
            grads_record[side],
            narrow_record[side],
            far=side == 0,
        )
        mats_even = moved if side == 0 else mats_even
        returned = exchange(target)
        values = row_record[side]
        if side == 1 and layer > 1:
            grads, sending = turn_back(returned, routing[layer], values, grads, routing[layer - 1])
        else:
            grads = take_back(returned, routing[layer], values, grads)
        if layer == section_count - 1:
            parts, sending = lax.optimization_barrier((parts, sending))
            share = lax.psum_scatter(
                parts.reshape(-1, parts.shape[-1]), "expert", scatter_dimension=0, tiled=True
            ).reshape(parts.shape[1:])
        if layer == 2:
            share, grads = lax.optimization_barrier((share, grads))
            share = lax.all_to_all(share, "section", split_axis=0, concat_axis=0, tiled=True)
        if layer % 2 == 0:
            grads = hop(grads, layer - 2)
            sending = send_back(grads, routing[layer - 1])

    all_grads = jnp.concatenate([grads, lax.ppermute(grads, "section", to_even)], axis=0)
    saved = tuple(zip(kept_record, grads_record, narrow_record))
    theirs = tuple(swap(jnp.where(is_even, b, a)) for a, b in zip(*saved))
    held = tuple(jnp.where(is_even, a, b) for a, b in zip(*saved))
    joint = (kept_all,) + tuple(
        serve_last(exchange(send_back(all_grads, route_all)), pre_all, own[2])
    )
    sums = weight_sums(on_first, *zip(joint, held, theirs))
    share = jnp.sum(share[2 * last_pair :].astype(jnp.float32), axis=0)
    return (
        sums[0][None, None],
        sums[1][None, None],
        sums[2][None, None],
        share[0][None],
        share[1].T[None],
    )


def solution(mesh):
    return jax.shard_map(
        local,
        mesh=mesh,
        in_specs=(
            P(None, "expert", None),
            P(None, "expert"),
            P("section", None, "expert", None),
            P("section", None, "expert"),
            P("section", "expert", None, None),
            P("section", "expert", None, None),
            P("section", "expert", None, None),
            P("section", None, None),
            P("section", None, None),
            P(),
        ),
        out_specs=(
            P("section", "expert", None, None),
            P("section", "expert", None, None),
            P("section", "expert", None, None),
            P("section", "expert", None),
            P("section", None, "expert"),
        ),
        check_vma=False,
    )
```

```python
import jax
import jax.numpy as jnp
from jax import lax
from jax.experimental import pallas as pl
from jax.experimental.pallas import tpu as pltpu
from jax.sharding import PartitionSpec as P

epsilon = 1e-06
capacity = 3


def dot(left, right):
    return jnp.dot(left, right, preferred_element_type=jnp.float32)


def dot_t(left, right):
    return lax.dot_general(left, right, (((1,), (1,)), ((), ())), preferred_element_type=jnp.float32)


def dot_tn(left, right):
    return lax.dot_general(left, right, (((0,), (0,)), ((), ())), preferred_element_type=jnp.float32)


def rms_scale(values):
    widened = values.astype(jnp.float32)
    return lax.rsqrt(jnp.mean(widened * widened, axis=-1, keepdims=True) + epsilon)


def norm_back(values, row_scale, grad_norm):
    widened = values.astype(jnp.float32)
    inner_mean = jnp.mean(grad_norm * widened, axis=-1, keepdims=True)
    return row_scale * grad_norm - widened * (row_scale * row_scale * row_scale) * inner_mean


def slot_of_rows(expert_ids, expert_count, stride, offset):
    chosen = (expert_ids[:, None] == jnp.arange(expert_count, dtype=jnp.int32)[None, :]).astype(
        jnp.int32
    )
    earlier = jnp.arange(expert_ids.shape[0])[:, None] > jnp.arange(expert_ids.shape[0])[None, :]
    same = expert_ids[:, None] == expert_ids[None, :]
    rank = jnp.sum((same & earlier).astype(jnp.int32), axis=1)
    return expert_ids * stride + offset + rank


def table_of(slots, slot_count):
    grid = jnp.arange(slot_count, dtype=jnp.int32)
    return (grid[:, None] == slots[None, :]).astype(jnp.bfloat16)


def run_kernel(
    body, out_shape, scratch, *operands, far=(), far_out=(), scalars=(), aliases={}, limit=16
):
    absent = [k for k, operand in enumerate(operands) if operand is None]
    if absent:
        count, inner_body = (len(operands), body)
        operands = [operand for operand in operands if operand is not None]
        shift = {
            k: k - sum(gone < k for gone in absent) for k in range(count) if k not in absent
        }
        far, scalars = (tuple(shift[k] for k in group if k in shift) for group in (far, scalars))
        aliases = {shift[k]: out for k, out in aliases.items() if k in shift}

        def body(*refs):
            refs = iter(refs)
            given = [None if k in absent else next(refs) for k in range(count)]
            inner_body(*given, *refs)

    everywhere = pl.BlockSpec(memory_space=pltpu.HBM)
    near = pl.BlockSpec(memory_space=pltpu.VMEM)
    small = pl.BlockSpec(memory_space=pltpu.SMEM)
    in_specs = [
        small if k in scalars else everywhere if k in far else near for k in range(len(operands))
    ]
    leaves, treedef = jax.tree.flatten(out_shape)
    leaves = [
        pltpu.HBM(leaf.shape, leaf.dtype) if k in far_out else leaf
        for k, leaf in enumerate(leaves)
    ]
    out_specs = [everywhere if k in far_out else near for k in range(len(leaves))]
    return pl.pallas_call(
        body,
        out_shape=jax.tree.unflatten(treedef, leaves),
        in_specs=in_specs,
        out_specs=jax.tree.unflatten(treedef, out_specs),
        scratch_shapes=scratch,
        input_output_aliases=aliases,
        compiler_params=pltpu.CompilerParams(vmem_limit_bytes=limit * 1024 * 1024),
    )(*operands)


def array(shape, dtype=jnp.bfloat16):
    return jax.ShapeDtypeStruct(shape, dtype)


def unpack_slots(source, rows):
    count, depth, _ = source.shape
    for index in range(count):
        rows[depth * index : depth * (index + 1), :] = source[index].astype(jnp.float32)


def pack_slots(rows, target):
    count, depth, _ = target.shape
    for index in range(count):
        target[index] = rows[depth * index : depth * (index + 1), :].astype(jnp.bfloat16)


def normed_rows(values):
    widened = values.astype(jnp.float32)
    return (widened * rms_scale(values)).astype(jnp.bfloat16)


def send_body(values, table, target, rows):
    rows[...] = dot(table[...], normed_rows(values[...]))
    pack_slots(rows, target)


def take_rows(returned, pick_table, values, gate, result, rows):
    unpack_slots(returned, rows)
    gathered = dot(pick_table[...], rows[...].astype(jnp.bfloat16))
    result[...] = (values[...].astype(jnp.float32) + gate[...] * gathered).astype(jnp.bfloat16)


def keep(flag, copies, begin):
    @pl.when(flag[0] == 1)
    def _():
        for copy in copies:
            copy.start() if begin else copy.wait()


def take_body(flag, returned, pick_table, values, gate, old, result, record, rows, done):
    copies = [pltpu.make_async_copy(values, record, done.at[0])]
    keep(flag, copies, True)
    take_rows(returned, pick_table, values, gate, result, rows)
    keep(flag, copies, False)


def turn_body(
    flag, returned, pick_table, values, gate, old, table, result, record, target, rows, done
):
    copies = [pltpu.make_async_copy(values, record, done.at[0])]
    keep(flag, copies, True)
    take_rows(returned, pick_table, values, gate, result, rows)
    send_body(result, table, target, rows)
    keep(flag, copies, False)


def send_back_body(grads, gate, table, target, rows):
    grad_out = (gate[...] * grads[...].astype(jnp.float32)).astype(jnp.bfloat16)
    rows[...] = dot(table[...], grad_out)
    pack_slots(rows, target)


def take_back_body(returned, pick_table, record, grads, result, rows, values, done):
    load = pltpu.make_async_copy(record, values, done.at[0])
    load.start()
    unpack_slots(returned, rows)
    grad_norm = dot(pick_table[...], rows[...].astype(jnp.bfloat16))
    load.wait()
    value = values[...]
    result[...] = (
        grads[...].astype(jnp.float32) + norm_back(value, rms_scale(value), grad_norm)
    ).astype(jnp.bfloat16)


def turn_back_body(
    returned, pick_table, record, grads, gate, table, result, target, rows, values, done
):
    take_back_body(returned, pick_table, record, grads, result, rows, values, done)
    send_back_body(result, gate, table, target, rows)


def serve_body(
    flag,
    received,
    gate_mat,
    up_mat,
    down_mat,
    old_kept,
    old_pre,
    served,
    kept_record,
    pre_record,
    rows,
    kept,
    pre,
    done,
    ready=lambda index: None,
):
    unpack_slots(received, rows)
    kept[...] = rows[...].astype(jnp.bfloat16)
    first = [pltpu.make_async_copy(kept, kept_record, done.at[0])]
    keep(flag, first, True)
    ready(0)
    pre[0] = dot(kept[...], gate_mat[...])
    ready(1)
    pre[1] = dot(kept[...], up_mat[...])
    second = [pltpu.make_async_copy(pre, pre_record, done.at[1])]
    keep(flag, second, True)
    gate = pre[0]
    hidden = (gate * jax.nn.sigmoid(gate) * pre[1]).astype(jnp.bfloat16)
    ready(2)
    rows[...] = dot(hidden, down_mat[...])
    pack_slots(rows, served)
    keep(flag, first + second, False)


def fetch(sources, targets, done):
    copies = [
        pltpu.make_async_copy(source, target, done.at[index])
        for index, (source, target) in enumerate(zip(sources, targets))
    ]
    for copy in copies:
        copy.start()
    return lambda index: copies[index].wait()


def serve_far_body(flag, received, *refs):
    sources, refs, mats, loaded = (refs[:3], refs[3:-4], refs[-4:-1], refs[-1])
    old, outs, work = (refs[:2], refs[2:5], refs[8:])
    ready = fetch(sources, mats, loaded)
    serve_body(flag, received, *mats, *old, *outs, *work, ready=ready)


def serve_back_far_body(flag, received, pre_record, *refs):
    sources, refs, mats, loaded = (refs[:3], refs[3:-4], refs[-4:-1], refs[-1])
    old, outs, work = (refs[:2], refs[2:5], refs[8:])
    ready = fetch(sources[::-1], mats[::-1], loaded)
    serve_back_body(flag, received, pre_record, *mats, *old, *outs, *work, ready=ready)


def serve_back_rows(received, load, pre, down_mat, slot_grads, narrow, rows, begin):
    load.start()
    unpack_slots(received, rows)
    slot_grads[...] = rows[...].astype(jnp.bfloat16)
    begin()
    grad_hidden = dot_t(slot_grads[...], down_mat[...])
    load.wait()
    gate = pre[0]
    up = pre[1]
    gate_sig = jax.nn.sigmoid(gate)
    gate_act = gate * gate_sig
    grad_gate = (grad_hidden * up * (gate_sig * (1.0 + gate * (1.0 - gate_sig)))).astype(
        jnp.bfloat16
    )
    grad_up = (grad_hidden * gate_act).astype(jnp.bfloat16)
    inner = gate.shape[1]
    narrow[:, :inner] = (gate_act * up).astype(jnp.bfloat16)
    narrow[:, inner : 2 * inner] = grad_gate
    narrow[:, 2 * inner :] = grad_up
    return (grad_gate, grad_up)


def serve_back_body(
    flag,
    received,
    pre_record,
    gate_mat,
    up_mat,
    down_mat,
    old_grads,
    old_narrow,
    target,
    grads_record,
    narrow_record,
    rows,
    pre,
    slot_grads,
    narrow,
    done,
    ready=lambda index: None,
):
    load = pltpu.make_async_copy(pre_record, pre, done.at[0])
    first = [pltpu.make_async_copy(slot_grads, grads_record, done.at[1])]
    grad_gate, grad_up = serve_back_rows(
        received,
        load,
        pre,
        down_mat,
        slot_grads,
        narrow,
        rows,
        lambda: (keep(flag, first, True), ready(0)),
    )
    ready(1)
    ready(2)
    second = [pltpu.make_async_copy(narrow, narrow_record, done.at[2])]
    keep(flag, second, True)
    rows[...] = dot_t(grad_gate, gate_mat[...]) + dot_t(grad_up, up_mat[...])
    pack_slots(rows, target)
    keep(flag, first + second, False)


def serve_last_body(received, pre_record, down_mat, slot_grads, narrow, rows, pre, done):
    load = pltpu.make_async_copy(pre_record, pre, done.at[0])
    serve_back_rows(received, load, pre, down_mat, slot_grads, narrow, rows, lambda: None)


def lowrank_body(
    flag,
    rows,
    far_in,
    targets,
    head,
    grads,
    far_normed,
    far_act,
    far_pre,
    far_grads,
    far_same,
    mats,
    all_normed,
    all_act,
    all_pre,
    all_grads,
    values,
    inner,
    scale,
    loaded,
    stored,
):
    count = mats.shape[0]
    live = flag[0].astype(jnp.float32)

    def load(index):
        return pltpu.make_async_copy(far_in.at[index], mats.at[index], loaded.at[index])

    def store(kind, index):
        near, far = (
            (all_normed, far_normed),
            (all_act, far_act),
            (all_pre, far_pre),
            (all_grads, far_grads),
        )[kind]
        return pltpu.make_async_copy(near.at[index], far.at[index], stored.at[kind, index])

    for index in reversed(range(count)):
        load(index).start()
    values[0] = rows[...]

    def forward(step, carry):
        index = count - 1 - step
        value = values[step]
        row_scale = rms_scale(value)
        normed = (value.astype(jnp.float32) * row_scale).astype(jnp.bfloat16)
        load(index).wait()
        inner_pre = dot(normed, mats[index, 0])
        act = (inner_pre * jax.nn.sigmoid(inner_pre)).astype(jnp.bfloat16)
        all_normed[index] = normed
        all_act[index] = (act.astype(jnp.float32) * live).astype(jnp.bfloat16)
        store(0, index).start()
        store(1, index).start()
        inner[index] = inner_pre
        scale[index] = row_scale
        values[step + 1] = (
            value.astype(jnp.float32) + dot_t(act, mats[index, 1])
        ).astype(jnp.bfloat16)
        return carry

    lax.fori_loop(0, count, forward, 0)
    final = values[count]
    row_scale = rms_scale(final)
    logits = row_scale * jnp.sum(final.astype(jnp.float32) * head[...], axis=1, keepdims=True)
    grad_logit = jax.nn.sigmoid(logits) - targets[...]
    grads[...] = norm_back(final, row_scale, grad_logit * head[...]).astype(jnp.bfloat16)

    def backward(index, carry):
        value = values[count - 1 - index]
        grad = grads[...]
        inner_pre = inner[index]
        inner_sig = jax.nn.sigmoid(inner_pre)
        grad_act = dot(grad, mats[index, 1])
        grad_pre = (grad_act * (inner_sig * (1.0 + inner_pre * (1.0 - inner_sig)))).astype(
            jnp.bfloat16
        )
        grad_norm = dot_t(grad_pre, mats[index, 0])
        all_pre[index] = (grad_pre.astype(jnp.float32) * live).astype(jnp.bfloat16)
        all_grads[index] = grad
        store(2, index).start()
        store(3, index).start()
        grads[...] = (
            grad.astype(jnp.float32) + norm_back(value, scale[index], grad_norm)
        ).astype(jnp.bfloat16)
        return carry

    lax.fori_loop(0, count, backward, 0)
    for index in range(count):
        for kind in range(4):
            store(kind, index).wait()


def lowrank_layers(flag, rows, mats, targets, head):
    count, rank = (mats.shape[0], mats.shape[3])
    row_count, width = rows.shape
    wide, narrow = ((count, row_count, width), (count, row_count, rank))
    return run_kernel(
        lowrank_body,
        (
            array(rows.shape),
            array(wide),
            array(narrow),
            array(narrow),
            array(wide),
            array(mats.shape),
        ),
        [
            pltpu.VMEM(mats.shape, jnp.bfloat16),
            pltpu.VMEM(wide, jnp.bfloat16),
            pltpu.VMEM(narrow, jnp.bfloat16),
            pltpu.VMEM(narrow, jnp.bfloat16),
            pltpu.VMEM(wide, jnp.bfloat16),
            pltpu.VMEM((count + 1, row_count, width), jnp.bfloat16),
            pltpu.VMEM((count, row_count, rank), jnp.float32),
            pltpu.VMEM((count, row_count, 1), jnp.float32),
            pltpu.SemaphoreType.DMA((count,)),
            pltpu.SemaphoreType.DMA((4, count)),
        ],
        flag,
        rows,
        mats,
        targets,
        head,
        far=(2,),
        far_out=(1, 2, 3, 4, 5),
        scalars=(0,),
        aliases={2: 5},
        limit=40,
    )[:5]


def parts_body(normed, pre, grads, act, parts):
    blocks, _, _, depth, rank = parts.shape
    for kind, (wide, narrow) in enumerate(((normed, pre), (grads, act))):
        part = dot_tn(wide[0], narrow[0]).astype(jnp.bfloat16)
        parts[:, 0, kind] = part.reshape(blocks, depth, rank)


def lowrank_sums(normed, pre, grads, act, blocks):
    count, row_count, width = normed.shape
    rank = pre.shape[2]
    wide = pl.BlockSpec((1, row_count, width), lambda k: (k, 0, 0))
    narrow = pl.BlockSpec((1, row_count, rank), lambda k: (k, 0, 0))
    depth = width // blocks
    return pl.pallas_call(
        parts_body,
        grid=(count,),
        out_shape=pltpu.HBM((blocks, count, 2, depth, rank), jnp.bfloat16),
        in_specs=[wide, narrow, wide, narrow],
        out_specs=pl.BlockSpec((blocks, 1, 2, depth, rank), lambda k: (0, k, 0, 0, 0)),
        compiler_params=pltpu.CompilerParams(vmem_limit_bytes=16 * 1024 * 1024),
        cost_estimate=pl.CostEstimate(
            flops=4 * count * row_count * width * rank,
            bytes_accessed=4 * count * width * (row_count + rank),
            transcendentals=0,
        ),
    )(normed, pre, grads, act)


def choose(flag, joint, mine, theirs, chosen):
    half = mine.shape[0]

    @pl.when(flag[0] == 1)
    def _():
        chosen[...] = joint[...]

    @pl.when(flag[0] != 1)
    def _():
        chosen[:half, :] = mine[...]
        chosen[half:, :] = theirs[...]


def weights_body(flag, *refs):
    sources, (gate, up, down), (kept, slot_grads, narrow) = (refs[:9], refs[9:12], refs[12:])
    choose(flag, *sources[0:3], kept)
    choose(flag, *sources[3:6], slot_grads)

    @pl.when(pl.program_id(0) == 0)
    def _():
        choose(flag, *sources[6:9], narrow)

    inner = gate.shape[1]
    gate[...] = dot_tn(kept[...], narrow[:, inner : 2 * inner])
    up[...] = dot_tn(kept[...], narrow[:, 2 * inner :])
    down[...] = dot_tn(narrow[:, :inner], slot_grads[...])


def weight_sums(flag, *triples):
    slots, width = triples[0][0].shape
    inner = triples[2][0].shape[1] // 3
    block = 2 * inner
    in_specs = [pl.BlockSpec(memory_space=pltpu.SMEM)]
    for triple in triples[:2]:
        in_specs += [pl.BlockSpec((part.shape[0], block), lambda k: (0, k)) for part in triple]
    in_specs += [pl.BlockSpec(part.shape, lambda k: (0, 0)) for part in triples[2]]
    tall = pl.BlockSpec((block, inner), lambda k: (k, 0))
    return pl.pallas_call(
        weights_body,
        grid=(width // block,),
        out_shape=tuple(
            jax.ShapeDtypeStruct(shape, jnp.float32)
            for shape in ((width, inner), (width, inner), (inner, width))
        ),
        in_specs=in_specs,
        out_specs=(tall, tall, pl.BlockSpec((inner, block), lambda k: (0, k))),
        scratch_shapes=[
            pltpu.VMEM((slots, block), jnp.bfloat16),
            pltpu.VMEM((slots, block), jnp.bfloat16),
            pltpu.VMEM((slots, 3 * inner), jnp.bfloat16),
        ],
        compiler_params=pltpu.CompilerParams(vmem_limit_bytes=16 * 1024 * 1024),
    )(flag, *(part for triple in triples for part in triple))


def exchange(buffer):
    return lax.all_to_all(buffer, "expert", split_axis=0, concat_axis=0, tiled=True)


def work_rows(slots, width):
    return [pltpu.VMEM((slots, width), jnp.float32)]


def packed_shape(table, width):
    count = lax.axis_size("expert")
    return array((count, table.shape[0] // count, width))


def send(values, table):
    width = values.shape[1]
    return run_kernel(
        send_body, packed_shape(table, width), work_rows(table.shape[0], width), values, table
    )


def take(flag, returned, route, values, record):
    table, pick_table, gate = route
    return run_kernel(
        take_body,
        (array(values.shape), array(values.shape)),
        work_rows(table.shape[0], values.shape[1]) + [pltpu.SemaphoreType.DMA((1,))],
        flag,
        returned,
        pick_table,
        values,
        gate,
        record,
        far=(5,),
        far_out=(1,),
        scalars=(0,),
        aliases={5: 1},
    )


def turn(flag, returned, route, values, record, next_table):
    table, pick_table, gate = route
    width = values.shape[1]
    return run_kernel(
        turn_body,
        (array(values.shape), array(values.shape), packed_shape(next_table, width)),
        work_rows(table.shape[0], width) + [pltpu.SemaphoreType.DMA((1,))],
        flag,
        returned,
        pick_table,
        values,
        gate,
        record,
        next_table,
        far=(5,),
        far_out=(1,),
        scalars=(0,),
        aliases={5: 1},
    )


def send_back(grads, route):
    table, _, gate = route
    width = grads.shape[1]
    return run_kernel(
        send_back_body,
        packed_shape(table, width),
        work_rows(table.shape[0], width),
        grads,
        gate,
        table,
    )


def load_rows(slots, values):
    return work_rows(slots, values.shape[1]) + [
        pltpu.VMEM(values.shape, jnp.bfloat16),
        pltpu.SemaphoreType.DMA((1,)),
    ]


def take_back(returned, route, values, grads):
    table, pick_table, _ = route
    return run_kernel(
        take_back_body,
        array(values.shape),
        load_rows(table.shape[0], values),
        returned,
        pick_table,
        values,
        grads,
        far=(2,),
    )


def turn_back(returned, route, values, grads, next_route):
    table, pick_table, _ = route
    return run_kernel(
        turn_back_body,
        (array(values.shape), packed_shape(next_route[0], values.shape[1])),
        load_rows(table.shape[0], values),
        returned,
        pick_table,
        values,
        grads,
        next_route[2],
        next_route[0],
        far=(2,),
    )


def far_mats(mats):
    return [pltpu.VMEM(mat.shape, mat.dtype) for mat in mats] + [pltpu.SemaphoreType.DMA((3,))]


def serve(flag, received, mats, kept, pre, far=False):
    count, depth, width = received.shape
    slots, inner = (count * depth, mats[0].shape[1])
    return run_kernel(
        serve_far_body if far else serve_body,
        (array(received.shape), array((slots, width)), array((2, slots, inner), jnp.float32))
        + (tuple(array(mat.shape) for mat in mats) if far else ()),
        work_rows(slots, width)
        + [
            pltpu.VMEM((slots, width), jnp.bfloat16),
            pltpu.VMEM((2, slots, inner), jnp.float32),
            pltpu.SemaphoreType.DMA((2,)),
        ]
        + (far_mats(mats) if far else []),
        flag,
        received,
        *mats,
        kept,
        pre,
        far=(2, 3, 4, 5, 6) if far else (5, 6),
        far_out=(1, 2, 3, 4, 5),
        scalars=(0,),
        aliases={2: 3, 3: 4, 4: 5, 5: 1, 6: 2} if far else {5: 1, 6: 2},
    )


def serve_back(flag, received, pre, mats, grads, narrow, far=False):
    width = received.shape[2]
    _, slots, inner = pre.shape
    return run_kernel(
        serve_back_far_body if far else serve_back_body,
        (array(received.shape), array((slots, width)), array((slots, 3 * inner)))
        + (tuple(array(mat.shape) for mat in mats) if far else ()),
        work_rows(slots, width)
        + [
            pltpu.VMEM(pre.shape, jnp.float32),
            pltpu.VMEM((slots, width), jnp.bfloat16),
            pltpu.VMEM((slots, 3 * inner), jnp.bfloat16),
            pltpu.SemaphoreType.DMA((3,)),
        ]
        + (far_mats(mats) if far else []),
        flag,
        received,
        pre,
        *mats,
        grads,
        narrow,
        far=(2, 3, 4, 5, 6, 7) if far else (2, 6, 7),
        far_out=(1, 2, 3, 4, 5),
        scalars=(0,),
        aliases={3: 3, 4: 4, 5: 5, 6: 1, 7: 2} if far else {6: 1, 7: 2},
    )


def serve_last(received, pre, down_mat):
    width = received.shape[2]
    _, slots, inner = pre.shape
    return run_kernel(
        serve_last_body,
        (array((slots, width)), array((slots, 3 * inner))),
        work_rows(slots, width)
        + [pltpu.VMEM(pre.shape, jnp.float32), pltpu.SemaphoreType.DMA((1,))],
        received,
        pre,
        down_mat,
        far=(1,),
    )


def local(
    features,
    labels,
    routes,
    route_gates,
    gate_weight,
    up_weight,
    down_weight,
    lowrank_in,
    lowrank_out,
    head_weight,
):
    section_count = lax.axis_size("section")
    section = lax.axis_index("section")
    expert_count = lax.axis_size("expert")
    micro_count, row_count, width = features.shape
    is_even = section % 2 == 0
    pair = section // 2
    to_odd = [(s, s + 1) for s in range(0, section_count, 2)]
    to_even = [(s + 1, s) for s in range(0, section_count, 2)]

    def swap(value):
        return lax.ppermute(value, "section", to_odd + to_even)

    def hop(value, layer):
        first = 0 if layer % 4 < 2 else 2
        links = []
        for start in range(first, first + section_count, 4):
            for lower in (start, start + 1):
                low_end, high_end = (lower % section_count, (lower + 2) % section_count)
                links += [(low_end, high_end), (high_end, low_end)]
        half = value.shape[0] // 2
        parts = [lax.ppermute(part, "section", links) for part in (value[:half], value[half:])]
        return jnp.concatenate(parts, axis=0)

    own = (gate_weight[0, 0], up_weight[0, 0], down_weight[0, 0])
    gate_other, up_other = (swap(own[0]), swap(own[1]))

    ids = routes[0, :, :, 0]
    plan = jnp.concatenate([ids.astype(jnp.float32), route_gates[0]], axis=0)
    plan_other = swap(plan)

    def route_of(slots, slot_count, gates):
        table = table_of(slots, slot_count)
        grid = jnp.arange(slot_count, dtype=jnp.int32)
        pick_table = (slots[:, None] == grid[None, :]).astype(jnp.bfloat16)
        return (table, pick_table, gates[:, None])

    def pick(first, second):
        chosen = jnp.where(is_even, first, second)
        mine = jnp.where(is_even, chosen[0::2], chosen[1::2])
        slots = slot_of_rows(mine[0].astype(jnp.int32), expert_count, capacity, 0)
        return route_of(slots, expert_count * capacity, mine[1])

    route_even = pick(plan, plan_other)
    route_odd = pick(plan_other, plan)
    joint_slots = jnp.concatenate(
        [
            slot_of_rows(ids[m], expert_count, capacity * micro_count, capacity * m)
            for m in range(micro_count)
        ]
    )
    route_all = route_of(
        joint_slots, expert_count * capacity * micro_count, route_gates[0].reshape(-1)
    )

    flags = [(pair == layer // 2).astype(jnp.int32)[None] for layer in range(section_count)]
    always = jnp.ones((1,), jnp.int32)
    first_rows = features.reshape(-1, width)
    served, kept_all, pre_all = serve(
        always, exchange(send(first_rows, route_all[0])), own, None, None
    )
    targets = jnp.where(is_even, labels[0], labels[1]).astype(jnp.float32)[:, None]
    on_first = (section == 0).astype(jnp.int32)[None]
    served, route_all, route_even, route_odd, flags, targets, on_first = lax.optimization_barrier(
        (served, route_all, route_even, route_odd, flags, targets, on_first)
    )
    routing = [route_odd if layer % 2 else route_even for layer in range(section_count)]
    returned, gate_other, up_other = lax.optimization_barrier(
        (exchange(served), gate_other, up_other)
    )
    second_rows, _ = take(always, returned, route_all, first_rows, None)
    second_rows, late = lax.optimization_barrier((second_rows, own[2]))
    crossing = lax.ppermute(second_rows[row_count:], "section", to_odd)
    down_back = lax.ppermute(late, "section", to_even)
    rows = jnp.where(is_even, second_rows[:row_count], crossing)
    rows, late = lax.optimization_barrier((rows, own[2]))
    down_on = lax.ppermute(late, "section", to_odd)
    sending = send(rows, routing[1][0])
    sending, gate_other, up_other = lax.optimization_barrier((sending, gate_other, up_other))
    others = (gate_other, up_other)
    mats_odd = tuple(jnp.where(is_even, b, a) for a, b in zip(own, others + (down_back,)))

    row_record = [None, None]
    kept_record = [None, None]
    pre_record = [None, None]
    for layer in range(1, section_count):
        side = layer % 2
        served, kept_record[side], pre_record[side], *moved = serve(
            flags[layer],
            exchange(sending),
            mats_odd if side else mats_even,
            kept_record[side],
            pre_record[side],
            far=side == 0,
        )
        if side == 0:
            mats_even = moved
        returned = exchange(served)
        if side == 0:
            rows, row_record[side], sending = turn(
                flags[layer],
                returned,
                routing[layer],
                rows,
                row_record[side],
                routing[layer + 1][0],
            )
            if layer == 2:
                low_own = jnp.stack([lowrank_in[0], lowrank_out[0].T])
                low_own, rows = lax.optimization_barrier((low_own, rows))
                low_mats = lax.all_gather(low_own, "section")
        else:
            rows, row_record[side] = take(
                flags[layer], returned, routing[layer], rows, row_record[side]
            )
            if layer == 1:
                rows, down_on = lax.optimization_barrier((rows, down_on))
                on = others + (down_on,)
                mats_even = tuple(jnp.where(is_even, a, b) for a, b in zip(own, on))
            if layer < section_count - 1:
                rows = hop(rows, layer)
                sending = send(rows, routing[layer + 1][0])

    grads, low_normed, low_act, low_pre, low_grads = lowrank_layers(
        flags[-1], rows, low_mats, targets, head_weight[None, :]
    )
    sending = send_back(grads, routing[section_count - 1])
    sending, low_normed, low_act, low_pre, low_grads = lax.optimization_barrier(
        (sending, low_normed, low_act, low_pre, low_grads)
    )

    parts = lowrank_sums(low_normed, low_pre, low_grads, low_act, expert_count)
    last_pair = section_count // 2 - 1

    grads_record = [None, None]
    narrow_record = [None, None]
    for layer in reversed(range(1, section_count)):
        side = layer % 2
        target, grads_record[side], narrow_record[side], *moved = serve_back(
            flags[layer],
            exchange(sending),
            pre_record[side],
            mats_odd if side else mats_even,
            grads_record[side],
            narrow_record[side],
            far=side == 0,
        )
        mats_even = moved if side == 0 else mats_even
        returned = exchange(target)
        values = row_record[side]
        if side == 1 and layer > 1:
            grads, sending = turn_back(returned, routing[layer], values, grads, routing[layer - 1])
        else:
            grads = take_back(returned, routing[layer], values, grads)
        if layer == section_count - 1:
            parts, sending = lax.optimization_barrier((parts, sending))
            share = lax.psum_scatter(
                parts.reshape(-1, parts.shape[-1]), "expert", scatter_dimension=0, tiled=True
            ).reshape(parts.shape[1:])
        if layer == 2:
            share, grads = lax.optimization_barrier((share, grads))
            share = lax.all_to_all(share, "section", split_axis=0, concat_axis=0, tiled=True)
        if layer % 2 == 0:
            grads = hop(grads, layer - 2)
            sending = send_back(grads, routing[layer - 1])

    all_grads = jnp.concatenate([grads, lax.ppermute(grads, "section", to_even)], axis=0)
    saved = tuple(zip(kept_record, grads_record, narrow_record))
    theirs = tuple(swap(jnp.where(is_even, b, a)) for a, b in zip(*saved))
    held = tuple(jnp.where(is_even, a, b) for a, b in zip(*saved))
    joint = (kept_all,) + tuple(
        serve_last(exchange(send_back(all_grads, route_all)), pre_all, own[2])
    )
    sums = weight_sums(on_first, *zip(joint, held, theirs))
    share = jnp.sum(share[2 * last_pair :].astype(jnp.float32), axis=0)
    return (
        sums[0][None, None],
        sums[1][None, None],
        sums[2][None, None],
        share[0][None],
        share[1].T[None],
    )


def solution(mesh):
    return jax.shard_map(
        local,
        mesh=mesh,
        in_specs=(
            P(None, "expert", None),
            P(None, "expert"),
            P("section", None, "expert", None),
            P("section", None, "expert"),
            P("section", "expert", None, None),
            P("section", "expert", None, None),
            P("section", "expert", None, None),
            P("section", None, None),
            P("section", None, None),
            P(),
        ),
        out_specs=(
            P("section", "expert", None, None),
            P("section", "expert", None, None),
            P("section", "expert", None, None),
            P("section", "expert", None),
            P("section", None, "expert"),
        ),
        check_vma=False,
    )
```
